32 devices in a mesh: seq: 16 (over z, x, core), wshard: 2 (over y).
Axes of the slice: x: 2, y: 2, z: 4, core: 2. Of those that a mesh axis runs over, the one named last changes fastest.
Arguments:
- inputs: bfloat16 [8192, 640], P(('seq', 'wshard')), may hold values from -6 to 6
- doc_ids: int32 [8192], P(('seq', 'wshard')), may hold values from 0 to 2, never falling along the last dimension, each value on 1 to 4096 neighbouring positions
- w_query: bfloat16 [640, 1024], P('wshard'), may hold values from -0.25 to 0.25
- w_key: bfloat16 [640, 256], P('wshard'), may hold values from -0.25 to 0.25
- w_value: bfloat16 [640, 256], P('wshard'), may hold values from -0.25 to 0.25
- w_out: bfloat16 [1024, 640], P('wshard'), may hold values from -0.1875 to 0.1875
- w_gate: bfloat16 [640, 2048], P('wshard'), may hold values from -0.25 to 0.25
- w_up: bfloat16 [640, 2048], P('wshard'), may hold values from -0.25 to 0.25
- w_down: bfloat16 [2048, 640], P('wshard'), may hold values from -0.125 to 0.125
- gain_in: bfloat16 [640], P('wshard'), may hold values from -0.5 to 1
- gain_attn_post: bfloat16 [640], P('wshard'), may hold values from -0.5 to 1
- gain_ff_pre: bfloat16 [640], P('wshard'), may hold values from -0.5 to 1
- gain_ff_post: bfloat16 [640], P('wshard'), may hold values from -0.5 to 1
- gain_query: bfloat16 [256], P('wshard'), may hold values from -0.5 to 1
- gain_key: bfloat16 [256], P('wshard'), may hold values from -0.5 to 1
- cotangent: bfloat16 [8192, 640], P(('seq', 'wshard')), may hold values from -6 to 6
Outputs:
- layer_out: bfloat16 [8192, 640], P(('seq', 'wshard'))
- grad_inputs: float32 [8192, 640], P(('seq', 'wshard'))
- grad_w_query: float32 [640, 1024], P('wshard')
- grad_w_key: float32 [640, 256], P('wshard')
- grad_w_value: float32 [640, 256], P('wshard')
- grad_w_out: float32 [1024, 640], P('wshard')
- grad_w_gate: float32 [640, 2048], P('wshard')
- grad_w_up: float32 [640, 2048], P('wshard')
- grad_w_down: float32 [2048, 640], P('wshard')
- grad_gain_in: float32 [640], P('wshard')
- grad_gain_attn_post: float32 [640], P('wshard')
- grad_gain_ff_pre: float32 [640], P('wshard')
- grad_gain_ff_post: float32 [640], P('wshard')
- grad_gain_query: float32 [256], P('wshard')
- grad_gain_key: float32 [256], P('wshard')
The draws below stay inside these ranges and needn't reach their ends.
Inputs may be any that keep to these rules, and one draw needn't show every extreme that they name: `doc_ids`: document numbers never fall along the token stream; every document has 1 to 4096 tokens, one exactly 4096.
All inputs are finite; a program needn't handle non-finite values.
Results may differ from the reference program's by a relative error of at most 0.025.
Values may be sent and summed in bfloat16 or wider, within the bound.
A program may use at most 128 MiB of HBM per device.

```python
import math
import jax
import jax.numpy as jnp
import numpy as np
from jax import lax

D = 640
H = 4
HD = 256
FF = 2048
WINDOW = 512
TOK_DEV = 256
DOCS = 3
TOKENS = 8192
MOST_DOC = 4096
N_SEQ = 16
N_WSHARD = 2


def block_scale(own_key, extent, shards, least, high):
    level, own = 1.0, jax.random.fold_in(own_key, 6)
    for axis_at, shards_of in shards:
        steps = jnp.exp(jax.random.uniform(jax.random.fold_in(own, axis_at), (shards_of,), jnp.float32, least / len(shards), high / len(shards)))
        level = level * jnp.repeat(steps, extent[axis_at] // shards_of).reshape([-1 if axis == axis_at else 1 for axis in range(len(extent))])
    return level


def profile(number_of, total, reach, lean):
    portions = [(1 << 20) // math.isqrt(rank ** lean) + 1 for rank in range(2, number_of + 1)]
    spare, holding = total - reach - (number_of - 1), [1] * (number_of - 1)
    while spare > 0:
        movable = [i for i in range(number_of - 1) if holding[i] < reach]
        mass, budget = sum([portions[i] for i in movable]), spare
        for i in movable:
            addition = min(reach - holding[i], max(1, budget * portions[i] // mass), spare)
            holding[i] = holding[i] + addition
            spare = spare - addition
    return np.array([reach] + holding)


def ragged_sizes(own_key, number_of, total, reach, slope):
    if number_of == 2:
        one = jax.random.randint(own_key, (), max(1, total - reach), min(reach, total - 1) + 1)
        return jnp.stack([one, total - one])
    sizes = jnp.asarray(profile(number_of, total, reach, slope), jnp.int32)
    twos = (number_of - 1) // 2
    donor, taker = sizes[1:1 + 2 * twos:2], sizes[2:2 + 2 * twos:2]
    slack = jnp.minimum(donor - 1, reach - taker)
    passed = jax.random.randint(jax.random.fold_in(own_key, 1), (twos,), 0, 1 << 20) % (slack + 1)
    sizes = sizes.at[1:1 + 2 * twos:2].set(donor - passed).at[2:2 + 2 * twos:2].set(taker + passed)
    return sizes[jax.random.permutation(jax.random.fold_in(own_key, 2), number_of)]


def noise(own_key, extent, scale, limit, cuts=(), kind=jnp.bfloat16):
    values = jax.random.normal(own_key, extent, jnp.float32) * scale
    if len(cuts) > 0:
        values = block_scale(own_key, extent, cuts, -0.22, 0.18) * values
    return jnp.clip(values, min=-limit, max=limit).astype(kind)


def setup_inputs(seed: int = 0) -> dict:
    streams_of = jax.random.split(jax.random.key(seed), 17)
    return {
        "inputs": noise(streams_of[0], (TOKENS, D), 1.0, 6.0, ((0, 32),)),
        "doc_ids": jnp.searchsorted(jnp.cumsum(ragged_sizes(streams_of[1], DOCS, TOKENS, MOST_DOC, 0)), jnp.arange(TOKENS), side="right").astype(jnp.int32),
        "w_query": noise(streams_of[2], (D, H * HD), D ** -0.5, 0.25, ((0, 2),)),
        "w_key": noise(streams_of[3], (D, HD), D ** -0.5, 0.25, ((0, 2),)),
        "w_value": noise(streams_of[4], (D, HD), D ** -0.5, 0.25, ((0, 2),)),
        "w_out": noise(streams_of[5], (H * HD, D), (H * HD) ** -0.5, 0.1875, ((0, 2),)),
        "w_gate": noise(streams_of[6], (D, FF), D ** -0.5, 0.25, ((0, 2),)),
        "w_up": noise(streams_of[7], (D, FF), D ** -0.5, 0.25, ((0, 2),)),
        "w_down": noise(streams_of[8], (FF, D), FF ** -0.5, 0.125, ((0, 2),)),
        "gain_in": jnp.clip(-0.5 + 1.5 * jax.random.uniform(streams_of[9], (D,), jnp.float32) ** block_scale(streams_of[9], (D,), ((0, 2),), -0.2, 0.2), -0.5, 1.0).astype(jnp.bfloat16),
        "gain_attn_post": jnp.clip(-0.5 + 1.5 * jax.random.uniform(streams_of[10], (D,), jnp.float32) ** block_scale(streams_of[10], (D,), ((0, 2),), -0.2, 0.2), -0.5, 1.0).astype(jnp.bfloat16),
        "gain_ff_pre": jnp.clip(-0.5 + 1.5 * jax.random.uniform(streams_of[11], (D,), jnp.float32) ** block_scale(streams_of[11], (D,), ((0, 2),), -0.2, 0.2), -0.5, 1.0).astype(jnp.bfloat16),
        "gain_ff_post": jnp.clip(-0.5 + 1.5 * jax.random.uniform(streams_of[12], (D,), jnp.float32) ** block_scale(streams_of[12], (D,), ((0, 2),), -0.2, 0.2), -0.5, 1.0).astype(jnp.bfloat16),
        "gain_query": jnp.clip(-0.5 + 1.5 * jax.random.uniform(streams_of[13], (HD,), jnp.float32) ** block_scale(streams_of[13], (HD,), ((0, 2),), -0.2, 0.2), -0.5, 1.0).astype(jnp.bfloat16),
        "gain_key": jnp.clip(-0.5 + 1.5 * jax.random.uniform(streams_of[14], (HD,), jnp.float32) ** block_scale(streams_of[14], (HD,), ((0, 2),), -0.2, 0.2), -0.5, 1.0).astype(jnp.bfloat16),
        "cotangent": noise(streams_of[15], (TOKENS, D), 1.0, 6.0, ((0, 32),)),
    }


NORM_EPSILON = 1e-06
ROPE_BASE = 10000.0
MASK_FLOOR = -1e+30

def rms_gain(tensor, gain_vec):
    factor = lax.rsqrt(lax.optimization_barrier(jnp.mean(tensor * tensor, axis=-1, keepdims=True)) + NORM_EPSILON)
    return tensor * factor * (1.0 + gain_vec)

def rope_tables(positions, head_width):
    half_width = head_width // 2
    exponent = jnp.arange(half_width, dtype=jnp.float32) * (2.0 / head_width)
    inverse = jnp.exp(-jnp.log(ROPE_BASE) * exponent)
    angles = positions.astype(jnp.float32)[:, None] * inverse[None, :]
    return (jnp.cos(angles), jnp.sin(angles))

def norm_rope(tensor, gain_vec, cos_table, sin_table):
    normed = rms_gain(tensor, gain_vec)
    half_width = tensor.shape[-1] // 2
    front_part = normed[..., :half_width]
    back_part = normed[..., half_width:]
    cos_rows = cos_table[:, None, :]
    sin_rows = sin_table[:, None, :]
    return jnp.concatenate([front_part * cos_rows - back_part * sin_rows, back_part * cos_rows + front_part * sin_rows], axis=-1)

def geglu(gate_pre, up_pre):
    return jax.nn.gelu(gate_pre, approximate=True) * up_pre

def window_mask(query_pos, key_pos, query_doc, key_doc):
    distance = query_pos[:, None] - key_pos[None, :]
    return (distance >= 0) & (distance < WINDOW) & (key_pos[None, :] >= 0) & (query_doc[:, None] == key_doc[None, :])

def log_totals(scores, allowed):
    row_peak = lax.optimization_barrier(jnp.max(scores, axis=-1, keepdims=True))
    row_total = lax.optimization_barrier(jnp.sum(jnp.where(allowed[None], jnp.exp(scores - row_peak), 0.0), axis=-1, keepdims=True))
    return row_peak + jnp.log(row_total)

def round_bf16(tensor):
    return lax.optimization_barrier(tensor.astype(jnp.bfloat16)).astype(jnp.float32)

def device_gain(per_row):
    device_count = N_SEQ * N_WSHARD
    parts = lax.optimization_barrier(jnp.sum(per_row.reshape(device_count, -1, per_row.shape[-1]), axis=1))
    return lax.optimization_barrier(jnp.sum(round_bf16(parts), axis=0))

def rms_pull(tensor, gain_vec, grad_out):
    _, pullback = jax.vjp(rms_gain, tensor, jnp.broadcast_to(gain_vec, tensor.shape))
    grad_tensor, grad_gain_rows = pullback(grad_out)
    return (grad_tensor, device_gain(grad_gain_rows))

def reference(inputs, doc_ids, w_query, w_key, w_value, w_out, w_gate, w_up, w_down, gain_in, gain_attn_post, gain_ff_pre, gain_ff_post, gain_query, gain_key, cotangent):
    token_count = inputs.shape[0]
    block_count = token_count // WINDOW
    device_count = N_SEQ * N_WSHARD
    score_scale = HD ** (-0.5)
    in_gain = gain_in.astype(jnp.float32)
    attn_post_gain = gain_attn_post.astype(jnp.float32)
    ff_pre_gain = gain_ff_pre.astype(jnp.float32)
    ff_post_gain = gain_ff_post.astype(jnp.float32)
    query_gain = gain_query.astype(jnp.float32)
    key_gain = gain_key.astype(jnp.float32)
    x_float = inputs.astype(jnp.float32)
    positions = jnp.arange(token_count, dtype=jnp.int32)
    cos_table, sin_table = rope_tables(positions, HD)
    normed_in = rms_gain(x_float, in_gain).astype(jnp.bfloat16)
    query_raw = jnp.dot(normed_in, w_query, preferred_element_type=jnp.float32).reshape(token_count, H, HD)
    key_raw = jnp.dot(normed_in, w_key, preferred_element_type=jnp.float32)[:, None, :]
    values = jnp.dot(normed_in, w_value, preferred_element_type=jnp.float32).astype(jnp.bfloat16)
    queries = norm_rope(query_raw, query_gain, cos_table, sin_table).astype(jnp.bfloat16)
    key_rot = norm_rope(key_raw, key_gain, cos_table, sin_table)[:, 0].astype(jnp.bfloat16)
    key_pad = jnp.concatenate([jnp.zeros((WINDOW, HD), jnp.bfloat16), key_rot], 0)
    value_pad = jnp.concatenate([jnp.zeros((WINDOW, HD), jnp.bfloat16), values], 0)
    doc_pad = jnp.concatenate([jnp.zeros((WINDOW,), jnp.int32), doc_ids], 0)

    def block_view(block_index):
        first_row = (block_index * WINDOW).astype(jnp.int32)
        block_queries = lax.dynamic_slice_in_dim(queries, first_row, WINDOW, 0)
        block_keys = lax.dynamic_slice_in_dim(key_pad, first_row, 2 * WINDOW, 0)
        block_values = lax.dynamic_slice_in_dim(value_pad, first_row, 2 * WINDOW, 0)
        query_pos = first_row + jnp.arange(WINDOW, dtype=jnp.int32)
        key_pos = first_row - WINDOW + jnp.arange(2 * WINDOW, dtype=jnp.int32)
        query_doc = lax.dynamic_slice_in_dim(doc_ids, first_row, WINDOW, 0)
        key_doc = lax.dynamic_slice_in_dim(doc_pad, first_row, 2 * WINDOW, 0)
        allowed = window_mask(query_pos, key_pos, query_doc, key_doc)
        scores = jnp.einsum('qhd,kd->hqk', block_queries.astype(jnp.float32), block_keys.astype(jnp.float32)) * score_scale
        scores = jnp.where(allowed[None], scores, MASK_FLOOR)
        return (block_queries, block_keys, block_values, allowed, scores)

    def forward_block(block_index):
        block_queries, block_keys, block_values, allowed, scores = block_view(block_index)
        log_total = log_totals(scores, allowed)
        soft = round_bf16(jnp.where(allowed[None], jnp.exp(scores - log_total), 0.0))
        mixed = jnp.einsum('hqk,kd->qhd', soft, block_values.astype(jnp.float32))
        return (mixed.reshape(WINDOW, H * HD).astype(jnp.bfloat16), log_total)
    block_ids = jnp.arange(block_count, dtype=jnp.int32)
    attn_blocks, log_blocks = lax.map(forward_block, block_ids)
    attended = attn_blocks.reshape(token_count, H * HD)
    attn_proj = jnp.dot(attended, w_out, preferred_element_type=jnp.float32)
    resid = x_float + rms_gain(attn_proj, attn_post_gain)
    normed_ff = rms_gain(resid, ff_pre_gain).astype(jnp.bfloat16)
    gate_pre = jnp.dot(normed_ff, w_gate, preferred_element_type=jnp.float32)
    up_pre = jnp.dot(normed_ff, w_up, preferred_element_type=jnp.float32)
    hidden = geglu(gate_pre, up_pre).astype(jnp.bfloat16)
    ff_proj = jnp.dot(hidden, w_down, preferred_element_type=jnp.float32)
    layer_out = (resid + rms_gain(ff_proj, ff_post_gain)).astype(jnp.bfloat16)
    grad_top = cotangent.astype(jnp.float32)
    grad_ff_proj, grad_gain_ff_post = rms_pull(ff_proj, ff_post_gain, grad_top)
    grad_ff_proj = grad_ff_proj.astype(jnp.bfloat16)
    grad_hidden = jnp.dot(grad_ff_proj, w_down.T, preferred_element_type=jnp.float32)
    _, pullback = jax.vjp(geglu, gate_pre, up_pre)
    grad_gate, grad_up = pullback(grad_hidden)
    grad_gate = grad_gate.astype(jnp.bfloat16)
    grad_up = grad_up.astype(jnp.bfloat16)
    grad_normed_ff = jnp.dot(grad_gate, w_gate.T, preferred_element_type=jnp.float32) + jnp.dot(grad_up, w_up.T, preferred_element_type=jnp.float32)
    grad_resid_part, grad_gain_ff_pre = rms_pull(resid, ff_pre_gain, grad_normed_ff)
    grad_resid = grad_top + grad_resid_part
    grad_attn_proj, grad_gain_attn_post = rms_pull(attn_proj, attn_post_gain, grad_resid)
    grad_attn_proj = grad_attn_proj.astype(jnp.bfloat16)
    grad_attended = jnp.dot(grad_attn_proj, w_out.T, preferred_element_type=jnp.float32).astype(jnp.bfloat16)
    grad_heads = grad_attended.reshape(token_count, H, HD)

    def backward_block(block_index):
        block_queries, block_keys, block_values, allowed, scores = block_view(block_index)
        first_row = (block_index * WINDOW).astype(jnp.int32)
        soft = jnp.where(allowed[None], jnp.exp(scores - log_blocks[block_index]), 0.0)
        block_grad = lax.dynamic_slice_in_dim(grad_heads, first_row, WINDOW, 0).astype(jnp.float32)
        grad_soft = jnp.einsum('qhd,kd->hqk', block_grad, block_values.astype(jnp.float32))
        row_inner = lax.optimization_barrier(jnp.sum(soft * grad_soft, axis=-1, keepdims=True))
        grad_score = round_bf16(soft * (grad_soft - row_inner) * score_scale)
        grad_query = jnp.einsum('hqk,kd->qhd', grad_score, block_keys.astype(jnp.float32))
        grad_key = jnp.einsum('hqk,qhd->kd', grad_score, block_queries.astype(jnp.float32))
        grad_value = jnp.einsum('hqk,qhd->kd', round_bf16(soft), block_grad)
        return (grad_query, grad_key, grad_value)
    grad_q_blocks, grad_k_blocks, grad_v_blocks = lax.map(backward_block, block_ids)
    grad_queries = grad_q_blocks.reshape(token_count, H, HD)
    spill_keys = jnp.concatenate([grad_k_blocks[1:, :WINDOW], jnp.zeros((1, WINDOW, HD), jnp.float32)], 0)
    spill_values = jnp.concatenate([grad_v_blocks[1:, :WINDOW], jnp.zeros((1, WINDOW, HD), jnp.float32)], 0)
    grad_keys = (grad_k_blocks[:, WINDOW:] + spill_keys).reshape(token_count, HD)
    grad_values = (grad_v_blocks[:, WINDOW:] + spill_values).reshape(token_count, HD).astype(jnp.bfloat16)

    def query_path(tensor, gain_full):
        return norm_rope(tensor, gain_full, cos_table, sin_table)
    _, pullback = jax.vjp(query_path, query_raw, jnp.broadcast_to(query_gain, query_raw.shape))
    grad_query_raw, grad_query_gain_rows = pullback(grad_queries)
    grad_gain_query = device_gain(grad_query_gain_rows)
    _, pullback = jax.vjp(query_path, key_raw, jnp.broadcast_to(key_gain, key_raw.shape))
    grad_key_raw, grad_key_gain_rows = pullback(grad_keys[:, None, :])
    grad_gain_key = device_gain(grad_key_gain_rows)
    grad_query_raw = grad_query_raw.reshape(token_count, H * HD).astype(jnp.bfloat16)
    grad_key_raw = grad_key_raw[:, 0].astype(jnp.bfloat16)
    grad_normed_in = jnp.dot(grad_query_raw, w_query.T, preferred_element_type=jnp.float32)
    grad_normed_in = grad_normed_in + jnp.dot(grad_key_raw, w_key.T, preferred_element_type=jnp.float32)
    grad_normed_in = grad_normed_in + jnp.dot(grad_values, w_value.T, preferred_element_type=jnp.float32)
    grad_input_part, grad_gain_in = rms_pull(x_float, in_gain, grad_normed_in)
    grad_inputs = grad_resid + grad_input_part
    pairs = ((normed_in, grad_query_raw), (normed_in, grad_key_raw), (normed_in, grad_values), (attended, grad_attn_proj), (normed_ff, grad_gate), (normed_ff, grad_up), (hidden, grad_ff_proj))
    stacked = tuple(((left.reshape(device_count, TOK_DEV, left.shape[-1]), right.reshape(device_count, TOK_DEV, right.shape[-1])) for left, right in pairs))
    initial = tuple((jnp.zeros((left.shape[-1], right.shape[-1]), jnp.float32) for left, right in pairs))

    def add_device(carry, pieces):
        updated = tuple((total + round_bf16(jnp.dot(piece[0].T, piece[1], preferred_element_type=jnp.float32)) for total, piece in zip(carry, pieces)))
        return (updated, None)
    weight_sums, _ = lax.scan(add_device, initial, stacked)
    grad_w_query, grad_w_key, grad_w_value, grad_w_out, grad_w_gate, grad_w_up, grad_w_down = weight_sums
    return (layer_out, grad_inputs, grad_w_query, grad_w_key, grad_w_value, grad_w_out, grad_w_gate, grad_w_up, grad_w_down, grad_gain_in, grad_gain_attn_post, grad_gain_ff_pre, grad_gain_ff_post, grad_gain_query, grad_gain_key)
```

```python
import functools
import types
import typing

import jax
import jax.numpy as jnp
from jax import lax
from jax.experimental import pallas as pl
from jax.experimental.pallas import tpu as pltpu
from jax.sharding import PartitionSpec as P

WINDOW = 512


NORM_EPSILON = 1e-06
ROPE_BASE = 10000.0
MASK_FLOOR = -1e30


def from_behind(array, axis, by):
    count = lax.axis_size(axis)
    pairs = [(i, i + by) for i in range(count) if 0 <= i + by < count]
    return lax.ppermute(array, axis, pairs)


def rms_gain(tensor, gain_vec):
    factor = lax.rsqrt(jnp.mean(tensor * tensor, axis=-1, keepdims=True) + NORM_EPSILON)
    return tensor * factor * (1.0 + gain_vec)


def rope_tables(positions, head_width):
    half_width = head_width // 2
    exponent = jnp.arange(half_width, dtype=jnp.float32) * (2.0 / head_width)
    inverse = jnp.exp(-jnp.log(ROPE_BASE) * exponent)
    angles = positions.astype(jnp.float32)[:, None] * inverse[None, :]
    return (jnp.cos(angles), jnp.sin(angles))


def norm_rope(tensor, gain_vec, cos_table, sin_table):
    normed = rms_gain(tensor, gain_vec)
    half_width = tensor.shape[-1] // 2
    front_part = normed[..., :half_width]
    back_part = normed[..., half_width:]
    cos_rows = cos_table[:, None, :]
    sin_rows = sin_table[:, None, :]
    return jnp.concatenate(
        [
            front_part * cos_rows - back_part * sin_rows,
            back_part * cos_rows + front_part * sin_rows,
        ],
        axis=-1,
    )


def geglu(gate_pre, up_pre):
    return jax.nn.gelu(gate_pre, approximate=True) * up_pre


def window_mask(query_pos, key_pos, query_doc, key_doc):
    distance = query_pos[:, None] - key_pos[None, :]
    return (
        (distance >= 0)
        & (distance < WINDOW)
        & (key_pos[None, :] >= 0)
        & (query_doc[:, None] == key_doc[None, :])
    )


def masked_scores(queries, all_keys, allowed, score_scale):
    scores = (
        jnp.einsum("qhd,kd->hqk", queries, all_keys, preferred_element_type=jnp.float32)
        * score_scale
    )
    return jnp.where(allowed[None], scores, MASK_FLOOR)


def weight_grad(left_rows, right_rows):
    return jnp.einsum("tc,tf->cf", left_rows, right_rows, preferred_element_type=jnp.float32)


MESH = pl.DeviceIdType.MESH
LANES = 128


def coordinates():
    seq = lax.axis_index("seq")
    return lax.rem(seq // 2, 2), lax.rem(seq, 2), seq // 4, lax.axis_index("wshard")


def device(x, core, z, y):
    return ((z * 2 + x) * 2 + core, y)


def greet(partners):
    barrier = pltpu.get_barrier_semaphore()
    for partner in partners:
        pl.semaphore_signal(barrier, inc=1, device_id=partner, device_id_type=MESH)
    pl.semaphore_wait(barrier, len(partners))


def remote(src, dst, send, recv, target):
    return pltpu.make_async_remote_copy(
        src_ref=src, dst_ref=dst, send_sem=send, recv_sem=recv,
        device_id=target, device_id_type=MESH,
    )


def token_dot(left, right):
    return lax.dot_general(
        left, right, (((0,), (0,)), ((), ())), preferred_element_type=jnp.float32
    ).astype(jnp.bfloat16)


GELU_SCALE = 0.7978845608028654
GELU_CUBE = 0.044715
GAIN_ROWS = 8
TERM_COLUMNS = 512


def dot(left, right):
    return jnp.dot(left, right, preferred_element_type=jnp.float32)


def dot_rows(left, right):
    return lax.dot_general(
        left, right, (((1,), (1,)), ((), ())), preferred_element_type=jnp.float32
    )


def dot_tokens(left, right):
    return lax.dot_general(
        left, right, (((0,), (0,)), ((), ())), preferred_element_type=jnp.float32
    )


def rms_factor(tensor):
    return lax.rsqrt(jnp.mean(tensor * tensor, axis=-1, keepdims=True) + NORM_EPSILON)


def rms_pull(tensor, gain_row, grad_out):
    factor = rms_factor(tensor)
    grad_normed = grad_out * (1.0 + gain_row)
    inner = jnp.mean(grad_normed * tensor, axis=-1, keepdims=True)
    grad_tensor = factor * grad_normed - tensor * (factor * factor * factor * inner)
    grad_gain = jnp.sum(grad_out * tensor * factor, axis=0, keepdims=True)
    return grad_tensor, grad_gain


def rotate(tensor, gain_row, cos_table, sin_table):
    half = tensor.shape[-1] // 2
    normed = tensor * rms_factor(tensor) * (1.0 + gain_row)
    front, back = normed[:, :half], normed[:, half:]
    return jnp.concatenate(
        [front * cos_table - back * sin_table, back * cos_table + front * sin_table], axis=-1
    )


def rotate_pull(tensor, gain_row, cos_table, sin_table, grad_out):
    half = tensor.shape[-1] // 2
    front, back = grad_out[:, :half], grad_out[:, half:]
    grad_normed = jnp.concatenate(
        [front * cos_table + back * sin_table, back * cos_table - front * sin_table], axis=-1
    )
    return rms_pull(tensor, gain_row, grad_normed)


def add_bf16(a, b):
    return (a.astype(jnp.float32) + b.astype(jnp.float32)).astype(jnp.bfloat16)


def lane_block(at, width):
    return pl.ds(pl.multiple_of(at * width, width), width)


class Weights(typing.NamedTuple):
    key: typing.Any
    value: typing.Any
    query: typing.Any
    out: typing.Any
    gate: typing.Any
    up: typing.Any
    down: typing.Any


class Inputs(typing.NamedTuple):
    x: typing.Any
    cotangent: typing.Any
    docs: typing.Any
    cos: typing.Any
    sin: typing.Any
    gains_own: typing.Any


class Outputs(typing.NamedTuple):
    layer_out: typing.Any
    grad_inputs: typing.Any
    summed: typing.Any
    gain_sums: typing.Any


class Sems(typing.NamedTuple):
    send: typing.Any
    recv: typing.Any


def layer_kernel(names, *refs):
    counts = [len(Inputs._fields), len(Weights._fields), len(Outputs._fields)]
    a, b, c = counts[0], counts[0] + counts[1], sum(counts)
    r = types.SimpleNamespace(**dict(zip(names, refs[c + counts[1] :])))
    for ref, name in zip(refs[:a] + refs[b:c], Inputs._fields + Outputs._fields):
        setattr(r, name, ref)
    shards, full = refs[a:b], Weights(*refs[c : c + counts[1]])
    x_ref, cot_ref, docs = r.x, r.cotangent, r.docs
    rows, dim = x_ref.shape
    head_dim = full.key.shape[1]
    heads = full.query.shape[1] // head_dim
    ff = full.gate.shape[1]
    score_scale = head_dim ** (-0.5)
    all_keys, all_values, halo_docs = r.all_keys, r.all_values, r.halo_docs
    hops = halo_docs.shape[0]
    span = hops * rows
    x, core, z, y = coordinates()
    depth = lax.axis_size("seq") // 4
    sibling = device(x, 1 - core, z, y)
    beside = device(1 - x, core, z, y)
    across = device(x, core, z, 1 - y)
    line = [device(x, core, lax.rem(z + d, depth), y) for d in range(1, depth)]
    width = lax.axis_size("wshard")
    total_devices = lax.axis_size("seq") * width
    me = lax.axis_index("seq") * width + lax.axis_index("wshard")

    def there(offset):
        return (me + offset >= 0) & (me + offset < total_devices)

    def neighbour(offset):
        place = lax.rem(me + offset + total_devices, total_devices)
        return (place // width, lax.rem(place, width))

    offsets = [d for d in range(-hops, hops + 1) if d != 0]
    greet([sibling, beside, across] + line + [neighbour(d) for d in offsets])

    half_ff = ff // 2
    items = [(0, None, 0, 1), (1, None, 0, 1), (2, None, 0, 1), (3, None, 0, 1)]
    for part in range(2):
        items += [(4, part, 0, 1), (5, part, 0, 1)]
    items += [(6, None, 0, 2), (6, None, 1, 2)]
    g_send, g_recv = r.g_send, r.g_recv

    def view(ref, low, high, part):
        if part is None:
            return ref.at[pl.ds(low, high)]
        return ref.at[pl.ds(low, high), pl.ds(part * half_ff, half_ff)]

    def geometry(i):
        name, part, piece, pieces = items[i]
        shard_rows = shards[name].shape[0]
        return name, part, shard_rows, shard_rows // 4, piece, shard_rows // 4 // pieces

    def first(i):
        name, part, shard_rows, quarter, piece, high = geometry(i)
        at = (core * 2 + x) * quarter + piece * high
        return remote(
            view(shards[name], at, high, part), view(full[name], y * shard_rows + at, high, part),
            g_send.at[0, i], g_recv.at[0, i], across,
        )

    def second(i):
        name, part, shard_rows, quarter, piece, high = geometry(i)
        at = (1 - y) * shard_rows + (core * 2 + x) * quarter + piece * high
        block = view(full[name], at, high, part)
        return remote(block, block, g_send.at[1, i], g_recv.at[1, i], beside)

    def third(i, side, slot):
        name, part, shard_rows, quarter, piece, high = geometry(i)
        at = (1 - y) * shard_rows + (core * 2 + side) * quarter + piece * high
        block = view(full[name], at, high, part)
        return remote(block, block, g_send.at[slot, i], g_recv.at[slot, i], sibling)

    def gain_gather():
        return remote(r.gains_own, r.gains_other, r.gain_gather_sems.at[0],
                      r.gain_gather_sems.at[1], across)

    def local(n):
        shard_rows = shards[n].shape[0]
        return pltpu.make_async_copy(
            shards[n], full[n].at[pl.ds(y * shard_rows, shard_rows)], r.own_sems.at[n]
        )

    def forward_one(i):
        first(i).wait_recv()
        second(i).start()
        third(i, x, 2).start()

    def forward_two(i):
        second(i).wait_recv()
        third(i, 1 - x, 3).start()

    def arrived(i):
        third(i, x, 2).wait_recv()
        third(i, 1 - x, 3).wait_recv()

    def shift_copy(k, d):
        slot = pl.ds((hops - d) * rows, rows)
        own = pl.ds(span, rows)
        if k == 0:
            src, dst = all_keys.at[own], all_keys.at[slot]
        elif k == 1:
            src, dst = all_values.at[own], all_values.at[slot]
        else:
            src, dst = docs, halo_docs.at[hops - d]
        return remote(src, dst, r.shift_send.at[k, d - 1], r.shift_recv.at[k, d - 1],
                      neighbour(d))

    def shift_start(kinds):
        for d in range(1, hops + 1):
            @pl.when(there(d))
            def _(d=d):
                for k in kinds:
                    shift_copy(k, d).start()

    def shift_arrive(kinds):
        for d in range(1, hops + 1):
            @pl.when(there(-d))
            def _(d=d):
                for k in kinds:
                    shift_copy(k, d).wait_recv()

            @pl.when(jnp.logical_not(there(-d)))
            def _(d=d):
                slot = slice((hops - d) * rows, (hops - d + 1) * rows)
                for k in kinds:
                    if k == 2:
                        halo_docs[hops - d] = jnp.zeros(docs.shape, docs.dtype)
                    else:
                        ref = (all_keys, all_values)[k]
                        ref[slot] = jnp.zeros((rows, head_dim), ref.dtype)

    gain_gather().start()
    for i in range(5):
        first(i).start()
    shift_start([2])
    for n in range(len(shards)):
        local(n).start()
    x_factor = rms_factor(x_ref[...].astype(jnp.float32))
    gain_gather().wait_recv()
    gains = r.gains
    gains[...] = r.gains_own[...] + r.gains_other[...]

    def gain(row, count=dim):
        return gains[row : row + 1, :count]

    normed_in = r.normed_in
    normed_in[...] = (
        x_ref[...].astype(jnp.float32) * x_factor * (1.0 + gain(0))
    ).astype(jnp.bfloat16)
    forward_one(0)
    forward_one(1)
    shift_arrive([2])
    bias = r.bias
    lane_tiles = docs.shape[0]
    query_docs = [
        jnp.transpose(jnp.broadcast_to(docs[k : k + 1].astype(jnp.float32), (LANES, LANES)))
        for k in range(lane_tiles)
    ]
    for block in range(lane_tiles * (hops + 1)):
        hop, k = block // lane_tiles, block % lane_tiles
        source = docs[k : k + 1] if hop == hops else halo_docs[hop, k : k + 1]
        key_docs = source.astype(jnp.float32)
        column = block * LANES + lax.broadcasted_iota(jnp.int32, (LANES, LANES), 1)
        for q in range(lane_tiles):
            row = q * LANES + lax.broadcasted_iota(jnp.int32, (LANES, LANES), 0)
            distance = row + span - column
            allowed = (
                (distance >= 0)
                & (distance < WINDOW)
                & (me * rows + column - span >= 0)
                & (query_docs[q] == key_docs)
            )
            bias[q * LANES : (q + 1) * LANES, block * LANES : (block + 1) * LANES] = jnp.where(
                allowed, 0.0, MASK_FLOOR
            )
    forward_one(2)
    forward_two(0)
    forward_two(1)
    for n in range(len(shards)):
        local(n).wait()
    arrived(0)
    arrived(1)
    key_raw = r.key_raw
    key_raw[...] = dot(normed_in[...], full.key[...])
    all_keys[span : span + rows] = rotate(
        key_raw[...], gain(5, head_dim), r.cos[...], r.sin[...]
    ).astype(jnp.bfloat16)
    all_values[span : span + rows] = dot(normed_in[...], full.value[...]).astype(jnp.bfloat16)
    shift_start([0, 1])
    for i in range(5, len(items)):
        first(i).start()
    forward_one(3)
    forward_two(2)
    arrived(2)
    query_raw, queries = r.query_raw, r.queries

    @pl.loop(0, heads)
    def _(h):
        at = lane_block(h, head_dim)
        raw = dot(normed_in[...], full.query[:, at])
        query_raw[:, at] = raw
        queries[:, at] = rotate(
            raw, gain(4, head_dim), r.cos[...], r.sin[...]
        ).astype(jnp.bfloat16)

    forward_one(4)
    forward_two(3)
    shift_arrive([0, 1])
    probs, attended = r.probs, r.attended

    def attend(h):
        at = lane_block(h, head_dim)
        scores = dot_rows(queries[:, at], all_keys[...]) * score_scale + bias[...]
        weights = jnp.exp(scores - jnp.max(scores, axis=-1, keepdims=True))
        weights = weights * (1.0 / jnp.sum(weights, axis=-1, keepdims=True))
        probs[h] = weights
        attended[:, at] = dot(weights.astype(jnp.bfloat16), all_values[...]).astype(jnp.bfloat16)

    half_heads = heads // 2
    pl.loop(0, half_heads)(attend)
    forward_one(5)
    forward_two(4)
    arrived(3)
    pl.loop(half_heads, heads)(attend)
    attn_proj, resid, normed_ff = r.attn_proj, r.resid, r.normed_ff
    attn_proj[...] = dot(attended[...], full.out[...])
    forward_one(6)
    forward_two(5)
    proj = attn_proj[...]
    resid[...] = x_ref[...].astype(jnp.float32) + proj * rms_factor(proj) * (1.0 + gain(1))
    res = resid[...]
    normed_ff[...] = (res * rms_factor(res) * (1.0 + gain(2))).astype(jnp.bfloat16)
    slope, act, hidden = r.slope, r.act, r.hidden
    ff_block = 512

    def expand(j):
        at = lane_block(j, ff_block)
        gate = dot(normed_ff[...], full.gate[:, at])
        up = dot(normed_ff[...], full.up[:, at])
        square = gate * gate
        tanh = jnp.tanh(GELU_SCALE * (gate + GELU_CUBE * (square * gate)))
        below = 0.5 * (1.0 + tanh)
        value = gate * below
        slope[:, at] = up * (
            below
            + (0.5 * GELU_SCALE) * gate * (1.0 - tanh * tanh) * (1.0 + 3.0 * GELU_CUBE * square)
        )
        act[:, at] = value
        hidden[:, at] = (value * up).astype(jnp.bfloat16)

    arrived(4)
    forward_one(7)
    forward_two(6)
    arrived(5)
    pl.loop(0, half_ff // ff_block)(expand)
    forward_one(8)
    forward_two(7)
    arrived(6)
    forward_one(9)
    forward_two(8)
    arrived(7)
    pl.loop(half_ff // ff_block, ff // ff_block)(expand)
    down_rows = shards[6].shape[0]
    ff_proj = r.ff_proj
    mine = lane_block(y, down_rows)
    ff_proj[...] = dot(hidden[:, mine], full.down[mine, :])
    forward_two(9)
    arrived(8)
    arrived(9)
    theirs = lane_block(1 - y, down_rows)
    proj = ff_proj[...] + dot(hidden[:, theirs], full.down[theirs, :])
    r.layer_out[...] = (
        resid[...] + proj * rms_factor(proj) * (1.0 + gain(3))
    ).astype(jnp.bfloat16)
    grad_gains = r.grad_gains
    grad_gains[...] = jnp.zeros_like(grad_gains)
    grad_ff_proj = r.grad_ff_proj
    grad_proj, grad_gain = rms_pull(proj, gain(3), cot_ref[...].astype(jnp.float32))
    grad_gains[3:4, :] = grad_gain
    grad_ff_proj[...] = grad_proj.astype(jnp.bfloat16)

    grad_gate, grad_up, accum = r.grad_gate, r.grad_up, ff_proj
    grad_resid, grad_attn_proj = resid, r.grad_attn_proj
    grad_keys, grad_values, grad_query = r.grad_keys, r.grad_values, r.grad_query
    grad_kv, back_send, back_recv = r.grad_kv, r.back_send, r.back_recv

    def task_hidden(j):
        at = lane_block(j, ff_block)
        grad_hidden = dot_rows(grad_ff_proj[...], full.down[at, :])
        grad_gate[:, at] = (grad_hidden * slope[:, at]).astype(jnp.bfloat16)
        grad_up[:, at] = (grad_hidden * act[:, at]).astype(jnp.bfloat16)

    def task_normed_ff(j):
        at = lane_block(j, ff_block)
        accum[...] += dot_rows(grad_gate[:, at], full.gate[:, at]) + dot_rows(
            grad_up[:, at], full.up[:, at]
        )

    def task_resid():
        part, grad_gain = rms_pull(resid[...], gain(2), accum[...])
        grad_gains[2:3, :] = grad_gain
        grad_resid[...] = cot_ref[...].astype(jnp.float32) + part
        grad_proj, grad_gain = rms_pull(attn_proj[...], gain(1), grad_resid[...])
        grad_gains[1:2, :] = grad_gain
        grad_attn_proj[...] = grad_proj.astype(jnp.bfloat16)
        grad_keys[...] = jnp.zeros_like(grad_keys)
        grad_values[...] = jnp.zeros_like(grad_values)

    def task_score(h):
        at = lane_block(h, head_dim)
        grad_head = dot_rows(grad_attn_proj[...], full.out[at, :]).astype(jnp.bfloat16)
        r.grad_head[...] = grad_head
        grad_soft = dot_rows(grad_head, all_values[...])
        weights = probs[h]
        inner = jnp.sum(weights * grad_soft, axis=-1, keepdims=True)
        r.grad_score[...] = (weights * (grad_soft - inner) * score_scale).astype(jnp.bfloat16)

    def task_head(h):
        at = lane_block(h, head_dim)
        grad_score = r.grad_score[...]
        grad_keys[...] += dot_tokens(grad_score, queries[:, at])
        grad_values[...] += dot_tokens(probs[h].astype(jnp.bfloat16), r.grad_head[...])
        grad_raw, grad_gain = rotate_pull(
            query_raw[:, at], gain(4, head_dim), r.cos[...], r.sin[...],
            dot(grad_score, all_keys[...]),
        )
        grad_gains[4:5, :head_dim] += grad_gain
        grad_query[:, at] = grad_raw.astype(jnp.bfloat16)

    def back_copy(k, d):
        slot = pl.ds((hops - d) * rows, rows)
        return remote(
            back_send.at[k, slot], back_recv.at[k, d - 1],
            r.back_shift_send.at[k, d - 1], r.back_shift_recv.at[k, d - 1], neighbour(-d),
        )

    def task_send_back():
        back_send[0] = grad_keys[:span].astype(jnp.bfloat16)
        back_send[1] = grad_values[:span].astype(jnp.bfloat16)
        for d in range(1, hops + 1):
            @pl.when(there(-d))
            def _(d=d):
                for k in range(2):
                    back_copy(k, d).start()

    def task_keys():
        for d in range(1, hops + 1):
            @pl.when(there(d))
            def _(d=d):
                for k in range(2):
                    back_copy(k, d).wait_recv()

            @pl.when(jnp.logical_not(there(d)))
            def _(d=d):
                for k in range(2):
                    back_recv[k, d - 1] = jnp.zeros((rows, head_dim), jnp.bfloat16)
        own_keys, own_values = grad_keys[span:], grad_values[span:]
        for d in range(1, hops + 1):
            own_keys = own_keys + back_recv[0, d - 1].astype(jnp.float32)
            own_values = own_values + back_recv[1, d - 1].astype(jnp.float32)
        grad_raw, grad_gain = rotate_pull(
            key_raw[...], gain(5, head_dim), r.cos[...], r.sin[...], own_keys
        )
        grad_gains[5:6, :head_dim] = grad_gain
        grad_kv[:, :head_dim] = grad_raw.astype(jnp.bfloat16)
        grad_kv[:, head_dim:] = own_values.astype(jnp.bfloat16)

    def task_inputs():
        grad_normed = (
            dot_rows(grad_query[...], full.query[...])
            + dot_rows(grad_kv[:, :head_dim], full.key[...])
            + dot_rows(grad_kv[:, head_dim:], full.value[...])
        )
        part, grad_gain = rms_pull(x_ref[...].astype(jnp.float32), gain(0), grad_normed)
        grad_gains[0:1, :] = grad_gain
        r.grad_inputs[...] = grad_resid[...] + part
        grad_gains[...] = grad_gains[...].astype(jnp.bfloat16).astype(jnp.float32)

    gain_in, gain_steps, gain_sums = r.gain_in, r.gain_steps, r.gain_sums

    def gain_copy(step):
        target = ([sibling, across, beside] + line)[step]
        src = grad_gains if step == 0 else gain_steps.at[min(step, 3) - 1]
        return remote(src, gain_in.at[step], r.send_gain.at[step], r.recv_gain.at[step], target)

    def task_gain(step):
        if step == 0:
            gain_copy(0).start()
        elif step <= 3:
            gain_copy(step - 1).wait_recv()
            before = grad_gains[...] if step == 1 else gain_steps[step - 2]
            gain_steps[step - 1] = before + gain_in[step - 1]
            if step < 3:
                gain_copy(step).start()
            else:
                for d in range(1, depth):
                    gain_copy(2 + d).start()
        else:
            total = gain_steps[2]
            for d in range(1, depth):
                gain_copy(2 + d).wait_recv()
                total = total + gain_in[2 + d]
            gain_sums[...] = total

    blocks = ff // ff_block
    accum[...] = jnp.zeros_like(accum)

    def tasks(t):
        @pl.when(t < blocks)
        def _():
            task_hidden(t)

        @pl.when((t >= 1) & (t <= blocks))
        def _():
            task_normed_ff(t - 1)

        at = blocks + 1
        pl.when(t == at)(task_resid)
        at += 1
        last = at + 2 * heads - 1

        @pl.when((t >= at) & (t <= last) & ((t - at) % 2 == 0))
        def _(at=at):
            task_score((t - at) // 2)

        @pl.when((t >= at) & (t <= last) & ((t - at) % 2 == 1))
        def _(at=at):
            task_head((t - at) // 2)

        pl.when(t == last)(task_send_back)
        pl.when(t == last + 2)(task_keys)
        pl.when(t == last + 3)(task_inputs)
        for step in range(5):
            pl.when(t == last + 4 + step)(functools.partial(task_gain, step))

    lefts = (hidden, normed_ff, normed_ff, attended, normed_in, normed_in)
    rights = (grad_ff_proj, grad_gate, grad_up, grad_attn_proj, grad_query, grad_kv)
    reduce_steps(r, lefts, rights, dim, depth, x, core, z, y, sibling, beside, across, line, tasks)

    gain_gather().wait_send()
    for i in range(len(items)):
        first(i).wait_send()
        second(i).wait_send()
        third(i, x, 2).wait_send()
        third(i, 1 - x, 3).wait_send()
    for d in range(1, hops + 1):
        @pl.when(there(d))
        def _(d=d):
            for k in range(3):
                shift_copy(k, d).wait_send()

        @pl.when(there(-d))
        def _(d=d):
            for k in range(2):
                back_copy(k, d).wait_send()
    for step in range(2 + depth):
        gain_copy(step).wait_send()


def term_groups(lefts, rights, dim, depth):
    groups = []
    for left, right in zip(lefts, rights):
        columns = right.shape[1]
        by_columns = columns % (depth * LANES) == 0
        piece = dim // 8 * LANES
        if by_columns:
            chunks = columns // (depth * LANES)
        else:
            chunks = left.shape[1] * columns // (8 * depth * piece)
        groups.append((left, right, by_columns, chunks))
    return groups


def reduce_steps(
    r, lefts, rights, dim, depth, x, core, z, y, sibling, beside, across, line, tasks
):
    terms, out = r.terms, r.summed
    from_core, from_across, from_beside, from_line = (
        r.from_core, r.from_across, r.from_beside, r.from_line
    )
    chunks = terms.shape[0]
    piece_rows = terms.shape[5]

    def to_core(c):
        send, recv = r.sem_core
        return remote(terms.at[c, 1 - core], from_core.at[c], send.at[c], recv.at[c], sibling)

    def to_across(c):
        send, recv = r.sem_across
        return remote(from_core.at[c, 1 - y], from_across.at[c], send.at[c], recv.at[c], across)

    def to_beside(c):
        send, recv = r.sem_beside
        return remote(from_across.at[c, 1 - x], from_beside.at[c], send.at[c], recv.at[c], beside)

    def to_line(c, d):
        send, recv = r.sem_line
        return remote(
            from_beside.at[c, lax.rem(z + d, depth)], from_line.at[c, d - 1],
            send.at[c, d - 1], recv.at[c, d - 1], line[d - 1],
        )

    def along_line(c, d, arrival=False):
        send, recv = r.sem_zline
        block = out.at[c, core, x, lax.rem(z + depth - d, depth) if arrival else z]
        return remote(block, block, send.at[c, d - 1], recv.at[c, d - 1], line[d - 1])

    def back_beside(c, side):
        send, recv = r.sem_xback
        block = out.at[c, core, side]
        return remote(block, block, send.at[c], recv.at[c], beside)

    def back_core(c, side):
        send, recv = r.sem_back
        block = out.at[c, side]
        return remote(block, block, send.at[c], recv.at[c], sibling)

    def make_columns(left, right, at, c):
        width = depth * LANES
        block = token_dot(left[...], right[:, lane_block(at, width)])
        for side in range(2):
            for own in range(2):
                for across_x in range(2):
                    low = ((side * 2 + own) * 2 + across_x) * piece_rows
                    for place in range(depth):
                        terms[c, own, side, across_x, place] = block[
                            low : low + piece_rows, place * LANES : (place + 1) * LANES
                        ]

    def make_rows(left, right, at, c, parts):
        rows, tiles = left.shape[1] // (2 * parts), right.shape[1] // LANES
        high = rows // (4 * depth)
        for side in range(2):
            start = pl.multiple_of((side * parts + at) * rows, rows)
            block = token_dot(left[:, pl.ds(start, rows)], right[...])
            for own in range(2):
                for across_x in range(2):
                    for place in range(depth):
                        low = ((own * 2 + across_x) * depth + place) * high
                        for tile in range(tiles):
                            terms[
                                c, own, side, across_x, place, tile * high : (tile + 1) * high
                            ] = block[low : low + high, tile * LANES : (tile + 1) * LANES]

    def make(t):
        start = 0
        for left, right, by_columns, parts in term_groups(lefts, rights, dim, depth):
            @pl.when((t >= start) & (t < start + parts))
            def _(left=left, right=right, by_columns=by_columns, parts=parts, start=start):
                if by_columns:
                    make_columns(left, right, t - start, t)
                else:
                    make_rows(left, right, t - start, t, parts)
            start += parts
        to_core(t).start()

    def stage(at, action):
        @pl.when((at >= 0) & (at < chunks))
        def _():
            action(at)

    def after_core(c):
        to_core(c).wait_recv()
        from_core[c, 1 - y] = add_bf16(from_core[c, 1 - y], terms[c, core, 1 - y])
        to_across(c).start()
        from_core[c, y] = add_bf16(from_core[c, y], terms[c, core, y])

    def after_across(c):
        to_across(c).wait_recv()
        from_across[c, 1 - x] = add_bf16(from_across[c, 1 - x], from_core[c, y, 1 - x])
        to_beside(c).start()
        from_across[c, x] = add_bf16(from_across[c, x], from_core[c, y, x])

    def after_beside(c):
        to_beside(c).wait_recv()
        from_beside[c] = add_bf16(from_beside[c], from_across[c, x])
        for d in range(1, depth):
            to_line(c, d).start()

    def after_line(c):
        total = from_beside[c, z].astype(jnp.float32)
        for d in range(1, depth):
            to_line(c, d).wait_recv()
            total = total + from_line[c, d - 1].astype(jnp.float32)
        out[c, core, x, z] = total.astype(jnp.bfloat16)
        for d in range(1, depth):
            along_line(c, d).start()

    def after_zline(c):
        for d in range(1, depth):
            along_line(c, d, True).wait_recv()
        back_beside(c, x).start()

    def after_xback(c):
        back_beside(c, 1 - x).wait_recv()
        back_core(c, core).start()

    actions = [make, after_core, after_across, after_beside, after_line, after_zline, after_xback]

    @pl.loop(0, chunks + len(actions) - 1)
    def _(t):
        for lag, action in enumerate(actions):
            stage(t - lag, action)
        tasks(t)

    @pl.loop(0, chunks)
    def _(c):
        back_core(c, 1 - core).wait_recv()
        to_core(c).wait_send()
        to_across(c).wait_send()
        to_beside(c).wait_send()
        for d in range(1, depth):
            to_line(c, d).wait_send()
            along_line(c, d).wait_send()
        back_beside(c, x).wait_send()
        back_core(c, core).wait_send()


def run_layer(x, cotangent, docs, cos_table, sin_table, gains_own, weights):
    rows, dim = x.shape
    depth = lax.axis_size("seq") // 4
    head_dim = weights.key.shape[1]
    inner = weights.query.shape[1]
    heads = inner // head_dim
    ff = weights.gate.shape[1]
    hops = WINDOW // rows
    keys = (hops + 1) * rows
    bf16, f32 = jnp.bfloat16, jnp.float32
    dma = pltpu.SemaphoreType.DMA
    chunks = (2 * inner * dim + 2 * dim * head_dim + 3 * dim * ff) // (dim * depth * LANES)
    piece = (dim // 8, LANES)
    item_count = 10
    gain_shape = (GAIN_ROWS, dim)
    pair = Sems(dma((chunks,)), dma((chunks,)))
    lines = Sems(dma((chunks, depth - 1)), dma((chunks, depth - 1)))
    fulls = [pltpu.VMEM((2 * w.shape[0], w.shape[1]), bf16) for w in weights]
    scratch = dict(
        gains_other=pltpu.VMEM(gain_shape, f32),
        gains=pltpu.VMEM(gain_shape, f32),
        halo_docs=pltpu.VMEM((hops,) + docs.shape, docs.dtype),
        bias=pltpu.VMEM((rows, keys), f32),
        normed_in=pltpu.VMEM((rows, dim), bf16),
        key_raw=pltpu.VMEM((rows, head_dim), f32),
        query_raw=pltpu.VMEM((rows, inner), f32),
        queries=pltpu.VMEM((rows, inner), bf16),
        all_keys=pltpu.VMEM((keys, head_dim), bf16),
        all_values=pltpu.VMEM((keys, head_dim), bf16),
        probs=pltpu.VMEM((heads, rows, keys), f32),
        attended=pltpu.VMEM((rows, inner), bf16),
        attn_proj=pltpu.VMEM((rows, dim), f32),
        resid=pltpu.VMEM((rows, dim), f32),
        normed_ff=pltpu.VMEM((rows, dim), bf16),
        slope=pltpu.VMEM((rows, ff), f32),
        act=pltpu.VMEM((rows, ff), f32),
        hidden=pltpu.VMEM((rows, ff), bf16),
        ff_proj=pltpu.VMEM((rows, dim), f32),
        grad_ff_proj=pltpu.VMEM((rows, dim), bf16),
        grad_gains=pltpu.VMEM(gain_shape, f32),
        grad_gate=pltpu.VMEM((rows, ff), bf16),
        grad_up=pltpu.VMEM((rows, ff), bf16),
        grad_attn_proj=pltpu.VMEM((rows, dim), bf16),
        grad_head=pltpu.VMEM((rows, head_dim), bf16),
        grad_score=pltpu.VMEM((rows, keys), bf16),
        grad_keys=pltpu.VMEM((keys, head_dim), f32),
        grad_values=pltpu.VMEM((keys, head_dim), f32),
        grad_query=pltpu.VMEM((rows, inner), bf16),
        grad_kv=pltpu.VMEM((rows, 2 * head_dim), bf16),
        back_send=pltpu.VMEM((2, hops * rows, head_dim), bf16),
        back_recv=pltpu.VMEM((2, hops, rows, head_dim), bf16),
        terms=pltpu.VMEM((chunks, 2, 2, 2, depth) + piece, bf16),
        from_core=pltpu.VMEM((chunks, 2, 2, depth) + piece, bf16),
        from_across=pltpu.VMEM((chunks, 2, depth) + piece, bf16),
        from_beside=pltpu.VMEM((chunks, depth) + piece, bf16),
        from_line=pltpu.VMEM((chunks, depth - 1) + piece, bf16),
        gain_in=pltpu.VMEM((2 + depth,) + gain_shape, f32),
        gain_steps=pltpu.VMEM((3,) + gain_shape, f32),
        gain_gather_sems=dma((2,)),
        own_sems=dma((len(weights),)),
        g_send=dma((4, item_count)),
        g_recv=dma((4, item_count)),
        shift_send=dma((3, hops)),
        shift_recv=dma((3, hops)),
        back_shift_send=dma((2, hops)),
        back_shift_recv=dma((2, hops)),
        send_gain=dma((2 + depth,)),
        recv_gain=dma((2 + depth,)),
        sem_core=pair,
        sem_across=pair,
        sem_beside=pair,
        sem_xback=pair,
        sem_back=pair,
        sem_line=lines,
        sem_zline=lines,
    )
    vmem = pl.BlockSpec(memory_space=pltpu.VMEM)
    return pl.pallas_call(
        functools.partial(layer_kernel, tuple(scratch)),
        out_shape=[
            jax.ShapeDtypeStruct((rows, dim), bf16),
            jax.ShapeDtypeStruct((rows, dim), f32),
            jax.ShapeDtypeStruct((chunks, 2, 2, depth) + piece, bf16),
            jax.ShapeDtypeStruct(gain_shape, f32),
        ],
        in_specs=[vmem] * 6 + [pl.BlockSpec(memory_space=pl.ANY)] * len(weights),
        out_specs=[vmem] * 4,
        scratch_shapes=fulls + list(scratch.values()),
        compiler_params=pltpu.CompilerParams(
            collective_id=1, has_side_effects=True, vmem_limit_bytes=67043328
        ),
        name="layer",
    )(x, cotangent, docs, cos_table, sin_table, gains_own, *weights)


def finish_kernel(plan, count, summed, layer_in, inputs_in, *refs):
    outs, layer_out, grad_inputs = refs[:count], refs[count], refs[count + 1]
    stages = refs[count + 2 : 2 * count + 2]
    chunk_sems, side_sems = refs[2 * count + 2 :]
    depth, rows = summed.shape[3], summed.shape[4]
    sides = [
        pltpu.make_async_copy(layer_in, layer_out, side_sems.at[0]),
        pltpu.make_async_copy(inputs_in, grad_inputs, side_sems.at[1]),
    ]
    for copy in sides:
        copy.start()

    def copies(group, at):
        outputs, by_columns, start, parts = group
        if len(outputs) > 1:
            return [
                pltpu.make_async_copy(stages[k], outs[k], chunk_sems.at[start + n])
                for n, k in enumerate(outputs)
            ]
        stage, out = stages[outputs[0]], outs[outputs[0]]
        if by_columns:
            view = (slice(None), lane_block(at, depth * LANES))
        else:
            high = stage.shape[0] // parts
            view = (pl.ds(pl.multiple_of(at * high, high), high),)
        return [pltpu.make_async_copy(stage.at[view], out.at[view], chunk_sems.at[start + at])]

    def convert(group, at):
        outputs, by_columns, start, parts = group
        stage = stages[outputs[0]]
        for core in range(2):
            for x in range(2):
                for z in range(depth):
                    piece = summed[start + at, core, x, z].astype(jnp.float32)
                    if by_columns:
                        low = (core * 2 + x) * rows
                        if len(outputs) > 1:
                            wide = stage.shape[1]
                            stage = stages[outputs[z * LANES // wide]]
                            place = pl.ds(z * LANES % wide, LANES)
                        else:
                            place = pl.ds(
                                pl.multiple_of(at * depth * LANES + z * LANES, LANES), LANES
                            )
                        stage[low : low + rows, place] = piece
                    else:
                        tiles = stage.shape[1] // LANES
                        high = rows // tiles
                        block = stage.shape[0] // parts
                        low = pl.multiple_of(
                            at * block + ((core * 2 + x) * depth + z) * high, high
                        )
                        for tile in range(tiles):
                            stage[pl.ds(low, high), tile * LANES : (tile + 1) * LANES] = piece[
                                tile * high : (tile + 1) * high
                            ]
        for copy in copies(group, at):
            copy.start()

    for group in plan:
        if group[3] == 1:
            convert(group, 0)
        else:
            pl.loop(0, group[3])(functools.partial(convert, group))
    for group in plan:
        for at in range(group[3]):
            for copy in copies(group, at):
                copy.wait()
    for copy in sides:
        copy.wait()


def finish(summed, layer_out, grad_inputs, shapes):
    chunks, _, _, depth, rows, lanes = summed.shape
    width = depth * lanes
    plan, start, index = [], 0, 0
    while index < len(shapes):
        high, wide = shapes[index]
        together = max(1, width // wide) if wide <= width and width % wide == 0 else 1
        by_columns = (wide * together) % width == 0
        if by_columns:
            parts = wide * together // width
        else:
            parts = high * wide // (4 * depth * rows * lanes)
        plan.append((list(range(index, index + together)), by_columns, start, parts))
        start += parts
        index += together
    vmem, anywhere = pl.BlockSpec(memory_space=pltpu.VMEM), pl.BlockSpec(memory_space=pl.ANY)
    results = [jax.ShapeDtypeStruct(shape, jnp.float32) for shape in shapes]
    return pl.pallas_call(
        functools.partial(finish_kernel, plan, len(shapes)),
        out_shape=results
        + [jax.ShapeDtypeStruct(a.shape, a.dtype) for a in (layer_out, grad_inputs)],
        in_specs=[vmem] * 3,
        out_specs=[anywhere] * (len(shapes) + 2),
        scratch_shapes=[pltpu.VMEM(shape, jnp.float32) for shape in shapes]
        + [pltpu.SemaphoreType.DMA((chunks + len(shapes),)), pltpu.SemaphoreType.DMA((2,))],
        compiler_params=pltpu.CompilerParams(vmem_limit_bytes=40 * 2**20),
        name="finish",
    )(summed, layer_out, grad_inputs)


def pack_gains(small, dim):
    me = lax.axis_index("wshard")
    row_at = lax.broadcasted_iota(jnp.int32, (GAIN_ROWS, dim), 0)
    packed = jnp.zeros((GAIN_ROWS, dim), jnp.float32)
    for row, vec in enumerate(small):
        n = vec.shape[0]
        vec = vec.astype(jnp.float32)
        spread = jnp.where(me == 0, jnp.pad(vec, (0, dim - n)), jnp.pad(vec, (n, dim - 2 * n)))
        wide = lax.broadcast_in_dim(spread, (GAIN_ROWS, dim), (1,))
        packed = jnp.where(row_at == row, wide, packed)
    return packed


def per_device(
    inputs, doc_ids, w_query, w_key, w_value, w_out, w_gate, w_up, w_down,
    gain_in, gain_attn_post, gain_ff_pre, gain_ff_post, gain_query, gain_key, cotangent,
):
    rows, dim = inputs.shape
    small = (gain_in, gain_attn_post, gain_ff_pre, gain_ff_post, gain_query, gain_key)
    start_row = lax.axis_index(("seq", "wshard")) * rows
    cos_table, sin_table = rope_tables(
        start_row + jnp.arange(rows, dtype=jnp.int32), w_key.shape[1]
    )
    layer_out, grad_inputs, summed, gain_sums = run_layer(
        inputs, cotangent, doc_ids.reshape(-1, LANES), cos_table, sin_table,
        pack_gains(small, dim), Weights(w_key, w_value, w_query, w_out, w_gate, w_up, w_down),
    )
    order = (w_down, w_gate, w_up, w_out, w_query, w_key, w_value)
    results = finish(summed, layer_out, grad_inputs, [w.shape for w in order])
    sum_down, sum_gate, sum_up, sum_out, sum_query, sum_key, sum_value = results[:7]
    layer_out, grad_inputs = results[7:]
    me = lax.axis_index("wshard")
    gain_outs = []
    for row, vec in enumerate(small):
        n = vec.shape[0]
        gain_outs.append(jnp.where(me == 0, gain_sums[row, :n], gain_sums[row, n : 2 * n]))
    return (
        layer_out, grad_inputs, sum_query, sum_key, sum_value, sum_out, sum_gate, sum_up, sum_down,
    ) + tuple(gain_outs)


def per_device_general(
    inputs,
    doc_ids,
    w_query,
    w_key,
    w_value,
    w_out,
    w_gate,
    w_up,
    w_down,
    gain_in,
    gain_attn_post,
    gain_ff_pre,
    gain_ff_post,
    gain_query,
    gain_key,
    cotangent,
):
    gathered = (
        lax.all_gather(w_query, "wshard", axis=0, tiled=True),
        lax.all_gather(w_key, "wshard", axis=0, tiled=True),
        lax.all_gather(w_value, "wshard", axis=0, tiled=True),
        lax.all_gather(w_out, "wshard", axis=0, tiled=True),
        lax.all_gather(w_gate, "wshard", axis=0, tiled=True),
        lax.all_gather(w_up, "wshard", axis=0, tiled=True),
        lax.all_gather(w_down, "wshard", axis=0, tiled=True),
        lax.all_gather(gain_in, "wshard", axis=0, tiled=True),
        lax.all_gather(gain_attn_post, "wshard", axis=0, tiled=True),
        lax.all_gather(gain_ff_pre, "wshard", axis=0, tiled=True),
        lax.all_gather(gain_ff_post, "wshard", axis=0, tiled=True),
        lax.all_gather(gain_query, "wshard", axis=0, tiled=True),
        lax.all_gather(gain_key, "wshard", axis=0, tiled=True),
    )
    full_query, full_key, full_value, full_out, full_gate, full_up, full_down = gathered[:7]
    in_gain, attn_post_gain, ff_pre_gain, ff_post_gain, query_gain, key_gain = [
        g.astype(jnp.float32) for g in gathered[7:]
    ]
    row_count = inputs.shape[0]
    head_dim = full_key.shape[1]
    head_count = full_query.shape[1] // head_dim
    score_scale = head_dim ** (-0.5)
    start_row = lax.axis_index(("seq", "wshard")) * row_count
    query_pos = start_row + jnp.arange(row_count, dtype=jnp.int32)
    cos_table, sin_table = rope_tables(query_pos, head_dim)
    x_float = inputs.astype(jnp.float32)
    normed_in = rms_gain(x_float, in_gain).astype(jnp.bfloat16)
    query_raw = jnp.dot(normed_in, full_query, preferred_element_type=jnp.float32).reshape(
        row_count, head_count, head_dim
    )
    key_raw = jnp.dot(normed_in, full_key, preferred_element_type=jnp.float32)[:, None, :]
    values = jnp.dot(normed_in, full_value, preferred_element_type=jnp.float32).astype(jnp.bfloat16)
    queries = norm_rope(query_raw, query_gain, cos_table, sin_table).astype(jnp.bfloat16)
    key_rot = norm_rope(key_raw, key_gain, cos_table, sin_table)[:, 0].astype(jnp.bfloat16)
    sent_rows = min(WINDOW, row_count)
    hop_count = WINDOW // sent_rows
    outgoing = (key_rot, values, doc_ids)
    halo_keys = []
    halo_values = []
    halo_docs = []
    for distance in range(hop_count, 0, -1):
        arrived = from_behind((outgoing[0], outgoing[1], outgoing[2]), ("seq", "wshard"), distance)
        halo_keys.append(arrived[0])
        halo_values.append(arrived[1])
        halo_docs.append(arrived[2])
    all_keys = jnp.concatenate(halo_keys + [key_rot], 0)
    all_values = jnp.concatenate(halo_values + [values], 0)
    all_docs = jnp.concatenate(halo_docs + [doc_ids], 0)
    key_pos = start_row - WINDOW + jnp.arange(WINDOW + row_count, dtype=jnp.int32)
    allowed = window_mask(query_pos, key_pos, doc_ids, all_docs)
    scores = masked_scores(queries, all_keys, allowed, score_scale)
    row_peak = jnp.max(scores, axis=-1, keepdims=True)
    row_total = jnp.sum(
        jnp.where(allowed[None], jnp.exp(scores - row_peak), 0.0), axis=-1, keepdims=True
    )
    log_total = row_peak + jnp.log(row_total)
    soft = jnp.where(allowed[None], jnp.exp(scores - log_total), 0.0).astype(jnp.bfloat16)
    attended = jnp.einsum("hqk,kd->qhd", soft, all_values, preferred_element_type=jnp.float32)
    attended = attended.reshape(row_count, head_count * head_dim).astype(jnp.bfloat16)
    attn_proj = jnp.dot(attended, full_out, preferred_element_type=jnp.float32)
    resid = x_float + rms_gain(attn_proj, attn_post_gain)
    normed_ff = rms_gain(resid, ff_pre_gain).astype(jnp.bfloat16)
    gate_pre = jnp.dot(normed_ff, full_gate, preferred_element_type=jnp.float32)
    up_pre = jnp.dot(normed_ff, full_up, preferred_element_type=jnp.float32)
    hidden = geglu(gate_pre, up_pre).astype(jnp.bfloat16)
    ff_proj = jnp.dot(hidden, full_down, preferred_element_type=jnp.float32)
    layer_out = (resid + rms_gain(ff_proj, ff_post_gain)).astype(jnp.bfloat16)
    grad_top = cotangent.astype(jnp.float32)
    _, pullback = jax.vjp(rms_gain, ff_proj, ff_post_gain)
    grad_ff_proj, grad_gain_ff_post = pullback(grad_top)
    grad_ff_proj = grad_ff_proj.astype(jnp.bfloat16)
    grad_w_down = weight_grad(hidden, grad_ff_proj)
    grad_hidden = lax.dot_general(
        grad_ff_proj, full_down, (((1,), (1,)), ((), ())), preferred_element_type=jnp.float32
    )
    _, pullback = jax.vjp(geglu, gate_pre, up_pre)
    grad_gate, grad_up = pullback(grad_hidden)
    grad_gate = grad_gate.astype(jnp.bfloat16)
    grad_up = grad_up.astype(jnp.bfloat16)
    grad_w_gate = weight_grad(normed_ff, grad_gate)
    grad_w_up = weight_grad(normed_ff, grad_up)
    grad_normed_ff = lax.dot_general(
        grad_gate, full_gate, (((1,), (1,)), ((), ())), preferred_element_type=jnp.float32
    )
    grad_normed_ff = grad_normed_ff + lax.dot_general(
        grad_up, full_up, (((1,), (1,)), ((), ())), preferred_element_type=jnp.float32
    )
    _, pullback = jax.vjp(rms_gain, resid, ff_pre_gain)
    grad_resid_part, grad_gain_ff_pre = pullback(grad_normed_ff)
    grad_resid = grad_top + grad_resid_part
    ff_gradients = (grad_w_gate, grad_w_up, grad_w_down, grad_gain_ff_pre, grad_gain_ff_post)
    ff_parts = (
        lax.psum_scatter(
            ff_gradients[0].astype(jnp.bfloat16), "wshard", scatter_dimension=0, tiled=True
        ).astype(jnp.float32),
        lax.psum_scatter(
            ff_gradients[1].astype(jnp.bfloat16), "wshard", scatter_dimension=0, tiled=True
        ).astype(jnp.float32),
        lax.psum_scatter(
            ff_gradients[2].astype(jnp.bfloat16), "wshard", scatter_dimension=0, tiled=True
        ).astype(jnp.float32),
        lax.psum_scatter(
            ff_gradients[3].astype(jnp.bfloat16), "wshard", scatter_dimension=0, tiled=True
        ).astype(jnp.float32),
        lax.psum_scatter(
            ff_gradients[4].astype(jnp.bfloat16), "wshard", scatter_dimension=0, tiled=True
        ).astype(jnp.float32),
    )
    ff_reduced = (
        lax.psum(ff_parts[0].astype(jnp.bfloat16), "seq").astype(jnp.float32),
        lax.psum(ff_parts[1].astype(jnp.bfloat16), "seq").astype(jnp.float32),
        lax.psum(ff_parts[2].astype(jnp.bfloat16), "seq").astype(jnp.float32),
        lax.psum(ff_parts[3].astype(jnp.bfloat16), "seq").astype(jnp.float32),
        lax.psum(ff_parts[4].astype(jnp.bfloat16), "seq").astype(jnp.float32),
    )
    _, pullback = jax.vjp(rms_gain, attn_proj, attn_post_gain)
    grad_attn_proj, grad_gain_attn_post = pullback(grad_resid)
    grad_attn_proj = grad_attn_proj.astype(jnp.bfloat16)
    grad_w_out = weight_grad(attended, grad_attn_proj)
    grad_attended = lax.dot_general(
        grad_attn_proj, full_out, (((1,), (1,)), ((), ())), preferred_element_type=jnp.float32
    ).astype(jnp.bfloat16)
    grad_heads = grad_attended.reshape(row_count, head_count, head_dim)
    again_scores = masked_scores(queries, all_keys, allowed, score_scale)
    probs = jnp.where(allowed[None], jnp.exp(again_scores - log_total), 0.0)
    grad_soft = jnp.einsum(
        "qhd,kd->hqk", grad_heads, all_values, preferred_element_type=jnp.float32
    )
    row_inner = jnp.sum(probs * grad_soft, axis=-1, keepdims=True)
    grad_score = (probs * (grad_soft - row_inner) * score_scale).astype(jnp.bfloat16)
    grad_queries = jnp.einsum(
        "hqk,kd->qhd", grad_score, all_keys, preferred_element_type=jnp.float32
    )
    grad_keys_all = jnp.einsum(
        "hqk,qhd->kd", grad_score, queries, preferred_element_type=jnp.float32
    )
    grad_values_all = jnp.einsum(
        "hqk,qhd->kd", probs.astype(jnp.bfloat16), grad_heads, preferred_element_type=jnp.float32
    )
    back_keys = jnp.zeros((sent_rows, head_dim), jnp.float32)
    back_values = jnp.zeros((sent_rows, head_dim), jnp.float32)
    for piece_index in range(hop_count):
        distance = hop_count - piece_index
        piece_start = piece_index * sent_rows
        arrived = (
            from_behind(
                grad_keys_all[piece_start : piece_start + sent_rows].astype(jnp.bfloat16),
                ("seq", "wshard"),
                -distance,
            ).astype(jnp.float32),
            from_behind(
                grad_values_all[piece_start : piece_start + sent_rows].astype(jnp.bfloat16),
                ("seq", "wshard"),
                -distance,
            ).astype(jnp.float32),
        )
        back_keys = back_keys + arrived[0]
        back_values = back_values + arrived[1]
    own_keys = grad_keys_all[WINDOW:]
    own_values = grad_values_all[WINDOW:]
    split_row = row_count - sent_rows
    grad_keys = jnp.concatenate([own_keys[:split_row], own_keys + back_keys], 0)
    grad_values = jnp.concatenate([own_values[:split_row], own_values + back_values], 0).astype(
        jnp.bfloat16
    )

    def query_path(tensor, gain_vec):
        return norm_rope(tensor, gain_vec, cos_table, sin_table)

    _, pullback = jax.vjp(query_path, query_raw, query_gain)
    grad_query_raw, grad_gain_query = pullback(grad_queries)
    _, pullback = jax.vjp(query_path, key_raw, key_gain)
    grad_key_raw, grad_gain_key = pullback(grad_keys[:, None, :])
    grad_query_raw = grad_query_raw.reshape(row_count, head_count * head_dim).astype(jnp.bfloat16)
    grad_key_raw = grad_key_raw[:, 0].astype(jnp.bfloat16)
    grad_w_query = weight_grad(normed_in, grad_query_raw)
    grad_w_key = weight_grad(normed_in, grad_key_raw)
    grad_w_value = weight_grad(normed_in, grad_values)
    grad_normed_in = lax.dot_general(
        grad_query_raw, full_query, (((1,), (1,)), ((), ())), preferred_element_type=jnp.float32
    )
    grad_normed_in = grad_normed_in + lax.dot_general(
        grad_key_raw, full_key, (((1,), (1,)), ((), ())), preferred_element_type=jnp.float32
    )
    grad_normed_in = grad_normed_in + lax.dot_general(
        grad_values, full_value, (((1,), (1,)), ((), ())), preferred_element_type=jnp.float32
    )
    _, pullback = jax.vjp(rms_gain, x_float, in_gain)
    grad_input_part, grad_gain_in = pullback(grad_normed_in)
    grad_inputs = grad_resid + grad_input_part
    attn_gradients = (
        grad_w_query,
        grad_w_key,
        grad_w_value,
        grad_w_out,
        grad_gain_in,
        grad_gain_attn_post,
        grad_gain_query,
        grad_gain_key,
    )
    attn_parts = (
        lax.psum_scatter(
            attn_gradients[0].astype(jnp.bfloat16), "wshard", scatter_dimension=0, tiled=True
        ).astype(jnp.float32),
        lax.psum_scatter(
            attn_gradients[1].astype(jnp.bfloat16), "wshard", scatter_dimension=0, tiled=True
        ).astype(jnp.float32),
        lax.psum_scatter(
            attn_gradients[2].astype(jnp.bfloat16), "wshard", scatter_dimension=0, tiled=True
        ).astype(jnp.float32),
        lax.psum_scatter(
            attn_gradients[3].astype(jnp.bfloat16), "wshard", scatter_dimension=0, tiled=True
        ).astype(jnp.float32),
        lax.psum_scatter(
            attn_gradients[4].astype(jnp.bfloat16), "wshard", scatter_dimension=0, tiled=True
        ).astype(jnp.float32),
        lax.psum_scatter(
            attn_gradients[5].astype(jnp.bfloat16), "wshard", scatter_dimension=0, tiled=True
        ).astype(jnp.float32),
        lax.psum_scatter(
            attn_gradients[6].astype(jnp.bfloat16), "wshard", scatter_dimension=0, tiled=True
        ).astype(jnp.float32),
        lax.psum_scatter(
            attn_gradients[7].astype(jnp.bfloat16), "wshard", scatter_dimension=0, tiled=True
        ).astype(jnp.float32),
    )
    attn_reduced = (
        lax.psum(attn_parts[0].astype(jnp.bfloat16), "seq").astype(jnp.float32),
        lax.psum(attn_parts[1].astype(jnp.bfloat16), "seq").astype(jnp.float32),
        lax.psum(attn_parts[2].astype(jnp.bfloat16), "seq").astype(jnp.float32),
        lax.psum(attn_parts[3].astype(jnp.bfloat16), "seq").astype(jnp.float32),
        lax.psum(attn_parts[4].astype(jnp.bfloat16), "seq").astype(jnp.float32),
        lax.psum(attn_parts[5].astype(jnp.bfloat16), "seq").astype(jnp.float32),
        lax.psum(attn_parts[6].astype(jnp.bfloat16), "seq").astype(jnp.float32),
        lax.psum(attn_parts[7].astype(jnp.bfloat16), "seq").astype(jnp.float32),
    )
    reduced = (
        attn_reduced[0],
        attn_reduced[1],
        attn_reduced[2],
        attn_reduced[3],
        ff_reduced[0],
        ff_reduced[1],
        ff_reduced[2],
        attn_reduced[4],
        attn_reduced[5],
        ff_reduced[3],
        ff_reduced[4],
        attn_reduced[6],
        attn_reduced[7],
    )
    return (layer_out, grad_inputs) + tuple(reduced)


def solution(mesh):
    routed = mesh.shape["wshard"] == 2 and mesh.shape["seq"] == 16
    return jax.shard_map(
        per_device if routed else per_device_general,
        mesh=mesh,
        in_specs=(
            P(("seq", "wshard"), None),
            P(("seq", "wshard")),
            P("wshard", None),
            P("wshard", None),
            P("wshard", None),
            P("wshard", None),
            P("wshard", None),
            P("wshard", None),
            P("wshard", None),
            P("wshard"),
            P("wshard"),
            P("wshard"),
            P("wshard"),
            P("wshard"),
            P("wshard"),
            P(("seq", "wshard"), None),
        ),
        out_specs=(
            P(("seq", "wshard"), None),
            P(("seq", "wshard"), None),
            P("wshard", None),
            P("wshard", None),
            P("wshard", None),
            P("wshard", None),
            P("wshard", None),
            P("wshard", None),
            P("wshard", None),
            P("wshard"),
            P("wshard"),
            P("wshard"),
            P("wshard"),
            P("wshard"),
            P("wshard"),
        ),
        check_vma=False,
    )
```

```python
import functools
import types
import typing

import jax
import jax.numpy as jnp
from jax import lax
from jax.experimental import pallas as pl
from jax.experimental.pallas import tpu as pltpu
from jax.sharding import PartitionSpec as P

WINDOW = 512


NORM_EPSILON = 1e-06
ROPE_BASE = 10000.0
MASK_FLOOR = -1e30


def from_behind(array, axis, by):
    count = lax.axis_size(axis)
    pairs = [(i, i + by) for i in range(count) if 0 <= i + by < count]
    return lax.ppermute(array, axis, pairs)


def rms_gain(tensor, gain_vec):
    factor = lax.rsqrt(jnp.mean(tensor * tensor, axis=-1, keepdims=True) + NORM_EPSILON)
    return tensor * factor * (1.0 + gain_vec)


def rope_tables(positions, head_width):
    half_width = head_width // 2
    exponent = jnp.arange(half_width, dtype=jnp.float32) * (2.0 / head_width)
    inverse = jnp.exp(-jnp.log(ROPE_BASE) * exponent)
    angles = positions.astype(jnp.float32)[:, None] * inverse[None, :]
    return (jnp.cos(angles), jnp.sin(angles))


def norm_rope(tensor, gain_vec, cos_table, sin_table):
    normed = rms_gain(tensor, gain_vec)
    half_width = tensor.shape[-1] // 2
    front_part = normed[..., :half_width]
    back_part = normed[..., half_width:]
    cos_rows = cos_table[:, None, :]
    sin_rows = sin_table[:, None, :]
    return jnp.concatenate(
        [
            front_part * cos_rows - back_part * sin_rows,
            back_part * cos_rows + front_part * sin_rows,
        ],
        axis=-1,
    )


def geglu(gate_pre, up_pre):
    return jax.nn.gelu(gate_pre, approximate=True) * up_pre


def window_mask(query_pos, key_pos, query_doc, key_doc):
    distance = query_pos[:, None] - key_pos[None, :]
    return (
        (distance >= 0)
        & (distance < WINDOW)
        & (key_pos[None, :] >= 0)
        & (query_doc[:, None] == key_doc[None, :])
    )


def masked_scores(queries, all_keys, allowed, score_scale):
    scores = (
        jnp.einsum("qhd,kd->hqk", queries, all_keys, preferred_element_type=jnp.float32)
        * score_scale
    )
    return jnp.where(allowed[None], scores, MASK_FLOOR)


def weight_grad(left_rows, right_rows):
    return jnp.einsum("tc,tf->cf", left_rows, right_rows, preferred_element_type=jnp.float32)


MESH = pl.DeviceIdType.MESH
LANES = 128


def coordinates():
    seq = lax.axis_index("seq")
    return lax.rem(seq // 2, 2), lax.rem(seq, 2), seq // 4, lax.axis_index("wshard")


def device(x, core, z, y):
    return ((z * 2 + x) * 2 + core, y)


def greet(partners):
    barrier = pltpu.get_barrier_semaphore()
    for partner in partners:
        pl.semaphore_signal(barrier, inc=1, device_id=partner, device_id_type=MESH)
    pl.semaphore_wait(barrier, len(partners))


def remote(src, dst, send, recv, target):
    return pltpu.make_async_remote_copy(
        src_ref=src, dst_ref=dst, send_sem=send, recv_sem=recv,
        device_id=target, device_id_type=MESH,
    )


def token_dot(left, right):
    return lax.dot_general(
        left, right, (((0,), (0,)), ((), ())), preferred_element_type=jnp.float32
    ).astype(jnp.bfloat16)


GELU_SCALE = 0.7978845608028654
GELU_CUBE = 0.044715
GAIN_ROWS = 8
TERM_COLUMNS = 512


def dot(left, right):
    return jnp.dot(left, right, preferred_element_type=jnp.float32)


def dot_rows(left, right):
    return lax.dot_general(
        left, right, (((1,), (1,)), ((), ())), preferred_element_type=jnp.float32
    )


def dot_tokens(left, right):
    return lax.dot_general(
        left, right, (((0,), (0,)), ((), ())), preferred_element_type=jnp.float32
    )


def rms_factor(tensor):
    return lax.rsqrt(jnp.mean(tensor * tensor, axis=-1, keepdims=True) + NORM_EPSILON)


def rms_pull(tensor, gain_row, grad_out):
    factor = rms_factor(tensor)
    grad_normed = grad_out * (1.0 + gain_row)
    inner = jnp.mean(grad_normed * tensor, axis=-1, keepdims=True)
    grad_tensor = factor * grad_normed - tensor * (factor * factor * factor * inner)
    grad_gain = jnp.sum(grad_out * tensor * factor, axis=0, keepdims=True)
    return grad_tensor, grad_gain


def rotate(tensor, gain_row, cos_table, sin_table):
    half = tensor.shape[-1] // 2
    normed = tensor * rms_factor(tensor) * (1.0 + gain_row)
    front, back = normed[:, :half], normed[:, half:]
    return jnp.concatenate(
        [front * cos_table - back * sin_table, back * cos_table + front * sin_table], axis=-1
    )


def rotate_pull(tensor, gain_row, cos_table, sin_table, grad_out):
    half = tensor.shape[-1] // 2
    front, back = grad_out[:, :half], grad_out[:, half:]
    grad_normed = jnp.concatenate(
        [front * cos_table + back * sin_table, back * cos_table - front * sin_table], axis=-1
    )
    return rms_pull(tensor, gain_row, grad_normed)


def add_bf16(a, b):
    return (a.astype(jnp.float32) + b.astype(jnp.float32)).astype(jnp.bfloat16)


def lane_block(at, width):
    return pl.ds(pl.multiple_of(at * width, width), width)


class Weights(typing.NamedTuple):
    key: typing.Any
    value: typing.Any
    query: typing.Any
    out: typing.Any
    gate: typing.Any
    up: typing.Any
    down: typing.Any


class Inputs(typing.NamedTuple):
    x: typing.Any
    cotangent: typing.Any
    docs: typing.Any
    cos: typing.Any
    sin: typing.Any
    gains_own: typing.Any


class Outputs(typing.NamedTuple):
    layer_out: typing.Any
    grad_inputs: typing.Any
    summed: typing.Any
    gain_sums: typing.Any


class Sems(typing.NamedTuple):
    send: typing.Any
    recv: typing.Any


def layer_kernel(names, *refs):
    counts = [len(Inputs._fields), len(Weights._fields), len(Outputs._fields)]
    a, b, c = counts[0], counts[0] + counts[1], sum(counts)
    r = types.SimpleNamespace(**dict(zip(names, refs[c + counts[1] :])))
    for ref, name in zip(refs[:a] + refs[b:c], Inputs._fields + Outputs._fields):
        setattr(r, name, ref)
    shards, full = refs[a:b], Weights(*refs[c : c + counts[1]])
    x_ref, cot_ref, docs = r.x, r.cotangent, r.docs
    rows, dim = x_ref.shape
    head_dim = full.key.shape[1]
    heads = full.query.shape[1] // head_dim
    ff = full.gate.shape[1]
    score_scale = head_dim ** (-0.5)
    all_keys, all_values, halo_docs = r.all_keys, r.all_values, r.halo_docs
    hops = halo_docs.shape[0]
    span = hops * rows
    x, core, z, y = coordinates()
    depth = lax.axis_size("seq") // 4
    sibling = device(x, 1 - core, z, y)
    beside = device(1 - x, core, z, y)
    across = device(x, core, z, 1 - y)
    line = [device(x, core, lax.rem(z + d, depth), y) for d in range(1, depth)]
    width = lax.axis_size("wshard")
    total_devices = lax.axis_size("seq") * width
    me = lax.axis_index("seq") * width + lax.axis_index("wshard")

    def there(offset):
        return (me + offset >= 0) & (me + offset < total_devices)

    def neighbour(offset):
        place = lax.rem(me + offset + total_devices, total_devices)
        return (place // width, lax.rem(place, width))

    offsets = [d for d in range(-hops, hops + 1) if d != 0]
    greet([sibling, beside, across] + line + [neighbour(d) for d in offsets])

    half_ff = ff // 2
    items = [(0, None, 0, 1), (1, None, 0, 1), (2, None, 0, 1), (3, None, 0, 1)]
    for part in range(2):
        items += [(4, part, 0, 1), (5, part, 0, 1)]
    items += [(6, None, 0, 2), (6, None, 1, 2)]
    g_send, g_recv = r.g_send, r.g_recv

    def view(ref, low, high, part):
        if part is None:
            return ref.at[pl.ds(low, high)]
        return ref.at[pl.ds(low, high), pl.ds(part * half_ff, half_ff)]

    def geometry(i):
        name, part, piece, pieces = items[i]
        shard_rows = shards[name].shape[0]
        return name, part, shard_rows, shard_rows // 4, piece, shard_rows // 4 // pieces

    def first(i):
        name, part, shard_rows, quarter, piece, high = geometry(i)
        at = (core * 2 + x) * quarter + piece * high
        return remote(
            view(shards[name], at, high, part), view(full[name], y * shard_rows + at, high, part),
            g_send.at[0, i], g_recv.at[0, i], across,
        )

    def second(i):
        name, part, shard_rows, quarter, piece, high = geometry(i)
        at = (1 - y) * shard_rows + (core * 2 + x) * quarter + piece * high
        block = view(full[name], at, high, part)
        return remote(block, block, g_send.at[1, i], g_recv.at[1, i], beside)

    def third(i, side, slot):
        name, part, shard_rows, quarter, piece, high = geometry(i)
        at = (1 - y) * shard_rows + (core * 2 + side) * quarter + piece * high
        block = view(full[name], at, high, part)
        return remote(block, block, g_send.at[slot, i], g_recv.at[slot, i], sibling)

    def gain_gather():
        return remote(r.gains_own, r.gains_other, r.gain_gather_sems.at[0],
                      r.gain_gather_sems.at[1], across)

    def local(n):
        shard_rows = shards[n].shape[0]
        return pltpu.make_async_copy(
            shards[n], full[n].at[pl.ds(y * shard_rows, shard_rows)], r.own_sems.at[n]
        )

    def forward_one(i):
        first(i).wait_recv()
        second(i).start()
        third(i, x, 2).start()

    def forward_two(i):
        second(i).wait_recv()
        third(i, 1 - x, 3).start()

    def arrived(i):
        third(i, x, 2).wait_recv()
        third(i, 1 - x, 3).wait_recv()

    def shift_copy(k, d):
        slot = pl.ds((hops - d) * rows, rows)
        own = pl.ds(span, rows)
        if k == 0:
            src, dst = all_keys.at[own], all_keys.at[slot]
        elif k == 1:
            src, dst = all_values.at[own], all_values.at[slot]
        else:
            src, dst = docs, halo_docs.at[hops - d]
        return remote(src, dst, r.shift_send.at[k, d - 1], r.shift_recv.at[k, d - 1],
                      neighbour(d))

    def shift_start(kinds):
        for d in range(1, hops + 1):
            @pl.when(there(d))
            def _(d=d):
                for k in kinds:
                    shift_copy(k, d).start()

    def shift_arrive(kinds):
        for d in range(1, hops + 1):
            @pl.when(there(-d))
            def _(d=d):
                for k in kinds:
                    shift_copy(k, d).wait_recv()

            @pl.when(jnp.logical_not(there(-d)))
            def _(d=d):
                slot = slice((hops - d) * rows, (hops - d + 1) * rows)
                for k in kinds:
                    if k == 2:
                        halo_docs[hops - d] = jnp.zeros(docs.shape, docs.dtype)
                    else:
                        ref = (all_keys, all_values)[k]
                        ref[slot] = jnp.zeros((rows, head_dim), ref.dtype)

    gain_gather().start()
    for i in range(5):
        first(i).start()
    shift_start([2])
    for n in range(len(shards)):
        local(n).start()
    x_factor = rms_factor(x_ref[...].astype(jnp.float32))
    gain_gather().wait_recv()
    gains = r.gains
    gains[...] = r.gains_own[...] + r.gains_other[...]

    def gain(row, count=dim):
        return gains[row : row + 1, :count]

    normed_in = r.normed_in
    normed_in[...] = (
        x_ref[...].astype(jnp.float32) * x_factor * (1.0 + gain(0))
    ).astype(jnp.bfloat16)
    forward_one(0)
    forward_one(1)
    shift_arrive([2])
    bias = r.bias
    lane_tiles = docs.shape[0]
    query_docs = [
        jnp.transpose(jnp.broadcast_to(docs[k : k + 1].astype(jnp.float32), (LANES, LANES)))
        for k in range(lane_tiles)
    ]
    for block in range(lane_tiles * (hops + 1)):
        hop, k = block // lane_tiles, block % lane_tiles
        source = docs[k : k + 1] if hop == hops else halo_docs[hop, k : k + 1]
        key_docs = source.astype(jnp.float32)
        column = block * LANES + lax.broadcasted_iota(jnp.int32, (LANES, LANES), 1)
        for q in range(lane_tiles):
            row = q * LANES + lax.broadcasted_iota(jnp.int32, (LANES, LANES), 0)
            distance = row + span - column
            allowed = (
                (distance >= 0)
                & (distance < WINDOW)
                & (me * rows + column - span >= 0)
                & (query_docs[q] == key_docs)
            )
            bias[q * LANES : (q + 1) * LANES, block * LANES : (block + 1) * LANES] = jnp.where(
                allowed, 0.0, MASK_FLOOR
            )
    forward_one(2)
    forward_two(0)
    forward_two(1)
    for n in range(len(shards)):
        local(n).wait()
    arrived(0)
    arrived(1)
    key_raw = r.key_raw
    key_raw[...] = dot(normed_in[...], full.key[...])
    all_keys[span : span + rows] = rotate(
        key_raw[...], gain(5, head_dim), r.cos[...], r.sin[...]
    ).astype(jnp.bfloat16)
    all_values[span : span + rows] = dot(normed_in[...], full.value[...]).astype(jnp.bfloat16)
    shift_start([0, 1])
    for i in range(5, len(items)):
        first(i).start()
    forward_one(3)
    forward_two(2)
    arrived(2)
    query_raw, queries = r.query_raw, r.queries

    @pl.loop(0, heads)
    def _(h):
        at = lane_block(h, head_dim)
        raw = dot(normed_in[...], full.query[:, at])
        query_raw[:, at] = raw
        queries[:, at] = rotate(
            raw, gain(4, head_dim), r.cos[...], r.sin[...]
        ).astype(jnp.bfloat16)

    forward_one(4)
    forward_two(3)
    shift_arrive([0, 1])
    probs, attended = r.probs, r.attended

    def attend(h):
        at = lane_block(h, head_dim)
        scores = dot_rows(queries[:, at], all_keys[...]) * score_scale + bias[...]
        weights = jnp.exp(scores - jnp.max(scores, axis=-1, keepdims=True))
        weights = weights * (1.0 / jnp.sum(weights, axis=-1, keepdims=True))
        probs[h] = weights
        attended[:, at] = dot(weights.astype(jnp.bfloat16), all_values[...]).astype(jnp.bfloat16)

    half_heads = heads // 2
    pl.loop(0, half_heads)(attend)
    forward_one(5)
    forward_two(4)
    arrived(3)
    pl.loop(half_heads, heads)(attend)
    attn_proj, resid, normed_ff = r.attn_proj, r.resid, r.normed_ff
    attn_proj[...] = dot(attended[...], full.out[...])
    forward_one(6)
    forward_two(5)
    proj = attn_proj[...]
    resid[...] = x_ref[...].astype(jnp.float32) + proj * rms_factor(proj) * (1.0 + gain(1))
    res = resid[...]
    normed_ff[...] = (res * rms_factor(res) * (1.0 + gain(2))).astype(jnp.bfloat16)
    slope, act, hidden = r.slope, r.act, r.hidden
    ff_block = 512

    def expand(j):
        at = lane_block(j, ff_block)
        gate = dot(normed_ff[...], full.gate[:, at])
        up = dot(normed_ff[...], full.up[:, at])
        square = gate * gate
        tanh = jnp.tanh(GELU_SCALE * (gate + GELU_CUBE * (square * gate)))
        below = 0.5 * (1.0 + tanh)
        value = gate * below
        slope[:, at] = up * (
            below
            + (0.5 * GELU_SCALE) * gate * (1.0 - tanh * tanh) * (1.0 + 3.0 * GELU_CUBE * square)
        )
        act[:, at] = value
        hidden[:, at] = (value * up).astype(jnp.bfloat16)

    arrived(4)
    forward_one(7)
    forward_two(6)
    arrived(5)
    pl.loop(0, half_ff // ff_block)(expand)
    forward_one(8)
    forward_two(7)
    arrived(6)
    forward_one(9)
    forward_two(8)
    arrived(7)
    pl.loop(half_ff // ff_block, ff // ff_block)(expand)
    down_rows = shards[6].shape[0]
    ff_proj = r.ff_proj
    mine = lane_block(y, down_rows)
    ff_proj[...] = dot(hidden[:, mine], full.down[mine, :])
    forward_two(9)
    arrived(8)
    arrived(9)
    theirs = lane_block(1 - y, down_rows)
    proj = ff_proj[...] + dot(hidden[:, theirs], full.down[theirs, :])
    r.layer_out[...] = (
        resid[...] + proj * rms_factor(proj) * (1.0 + gain(3))
    ).astype(jnp.bfloat16)
    grad_gains = r.grad_gains
    grad_gains[...] = jnp.zeros_like(grad_gains)
    grad_ff_proj = r.grad_ff_proj
    grad_proj, grad_gain = rms_pull(proj, gain(3), cot_ref[...].astype(jnp.float32))
    grad_gains[3:4, :] = grad_gain
    grad_ff_proj[...] = grad_proj.astype(jnp.bfloat16)

    grad_gate, grad_up, accum = r.grad_gate, r.grad_up, ff_proj
    grad_resid, grad_attn_proj = resid, r.grad_attn_proj
    grad_keys, grad_values, grad_query = r.grad_keys, r.grad_values, r.grad_query
    grad_kv, back_send, back_recv = r.grad_kv, r.back_send, r.back_recv

    def task_hidden(j):
        at = lane_block(j, ff_block)
        grad_hidden = dot_rows(grad_ff_proj[...], full.down[at, :])
        grad_gate[:, at] = (grad_hidden * slope[:, at]).astype(jnp.bfloat16)
        grad_up[:, at] = (grad_hidden * act[:, at]).astype(jnp.bfloat16)

    def task_normed_ff(j):
        at = lane_block(j, ff_block)
        accum[...] += dot_rows(grad_gate[:, at], full.gate[:, at]) + dot_rows(
            grad_up[:, at], full.up[:, at]
        )

    def task_resid():
        part, grad_gain = rms_pull(resid[...], gain(2), accum[...])
        grad_gains[2:3, :] = grad_gain
        grad_resid[...] = cot_ref[...].astype(jnp.float32) + part
        grad_proj, grad_gain = rms_pull(attn_proj[...], gain(1), grad_resid[...])
        grad_gains[1:2, :] = grad_gain
        grad_attn_proj[...] = grad_proj.astype(jnp.bfloat16)
        grad_keys[...] = jnp.zeros_like(grad_keys)
        grad_values[...] = jnp.zeros_like(grad_values)

    def task_score(h):
        at = lane_block(h, head_dim)
        grad_head = dot_rows(grad_attn_proj[...], full.out[at, :]).astype(jnp.bfloat16)
        r.grad_head[...] = grad_head
        grad_soft = dot_rows(grad_head, all_values[...])
        weights = probs[h]
        inner = jnp.sum(weights * grad_soft, axis=-1, keepdims=True)
        r.grad_score[...] = (weights * (grad_soft - inner) * score_scale).astype(jnp.bfloat16)

    def task_head(h):
        at = lane_block(h, head_dim)
        grad_score = r.grad_score[...]
        grad_keys[...] += dot_tokens(grad_score, queries[:, at])
        grad_values[...] += dot_tokens(probs[h].astype(jnp.bfloat16), r.grad_head[...])
        grad_raw, grad_gain = rotate_pull(
            query_raw[:, at], gain(4, head_dim), r.cos[...], r.sin[...],
            dot(grad_score, all_keys[...]),
        )
        grad_gains[4:5, :head_dim] += grad_gain
        grad_query[:, at] = grad_raw.astype(jnp.bfloat16)

    def back_copy(k, d):
        slot = pl.ds((hops - d) * rows, rows)
        return remote(
            back_send.at[k, slot], back_recv.at[k, d - 1],
            r.back_shift_send.at[k, d - 1], r.back_shift_recv.at[k, d - 1], neighbour(-d),
        )

    def task_send_back():
        back_send[0] = grad_keys[:span].astype(jnp.bfloat16)
        back_send[1] = grad_values[:span].astype(jnp.bfloat16)
        for d in range(1, hops + 1):
            @pl.when(there(-d))
            def _(d=d):
                for k in range(2):
                    back_copy(k, d).start()

    def task_keys():
        for d in range(1, hops + 1):
            @pl.when(there(d))
            def _(d=d):
                for k in range(2):
                    back_copy(k, d).wait_recv()

            @pl.when(jnp.logical_not(there(d)))
            def _(d=d):
                for k in range(2):
                    back_recv[k, d - 1] = jnp.zeros((rows, head_dim), jnp.bfloat16)
        own_keys, own_values = grad_keys[span:], grad_values[span:]
        for d in range(1, hops + 1):
            own_keys = own_keys + back_recv[0, d - 1].astype(jnp.float32)
            own_values = own_values + back_recv[1, d - 1].astype(jnp.float32)
        grad_raw, grad_gain = rotate_pull(
            key_raw[...], gain(5, head_dim), r.cos[...], r.sin[...], own_keys
        )
        grad_gains[5:6, :head_dim] = grad_gain
        grad_kv[:, :head_dim] = grad_raw.astype(jnp.bfloat16)
        grad_kv[:, head_dim:] = own_values.astype(jnp.bfloat16)

    def task_inputs():
        grad_normed = (
            dot_rows(grad_query[...], full.query[...])
            + dot_rows(grad_kv[:, :head_dim], full.key[...])
            + dot_rows(grad_kv[:, head_dim:], full.value[...])
        )
        part, grad_gain = rms_pull(x_ref[...].astype(jnp.float32), gain(0), grad_normed)
        grad_gains[0:1, :] = grad_gain
        r.grad_inputs[...] = grad_resid[...] + part
        grad_gains[...] = grad_gains[...].astype(jnp.bfloat16).astype(jnp.float32)

    gain_in, gain_steps, gain_sums = r.gain_in, r.gain_steps, r.gain_sums

    def gain_copy(step):
        target = ([sibling, across, beside] + line)[step]
        src = grad_gains if step == 0 else gain_steps.at[min(step, 3) - 1]
        return remote(src, gain_in.at[step], r.send_gain.at[step], r.recv_gain.at[step], target)

    def task_gain(step):
        if step == 0:
            gain_copy(0).start()
        elif step <= 3:
            gain_copy(step - 1).wait_recv()
            before = grad_gains[...] if step == 1 else gain_steps[step - 2]
            gain_steps[step - 1] = before + gain_in[step - 1]
            if step < 3:
                gain_copy(step).start()
            else:
                for d in range(1, depth):
                    gain_copy(2 + d).start()
        else:
            total = gain_steps[2]
            for d in range(1, depth):
                gain_copy(2 + d).wait_recv()
                total = total + gain_in[2 + d]
            gain_sums[...] = total

    blocks = ff // ff_block
    accum[...] = jnp.zeros_like(accum)

    def tasks(t):
        @pl.when(t < blocks)
        def _():
            task_hidden(t)

        @pl.when((t >= 1) & (t <= blocks))
        def _():
            task_normed_ff(t - 1)

        at = blocks + 1
        pl.when(t == at)(task_resid)
        at += 1
        last = at + 2 * heads - 1

        @pl.when((t >= at) & (t <= last) & ((t - at) % 2 == 0))
        def _(at=at):
            task_score((t - at) // 2)

        @pl.when((t >= at) & (t <= last) & ((t - at) % 2 == 1))
        def _(at=at):
            task_head((t - at) // 2)

        pl.when(t == last)(task_send_back)
        pl.when(t == last + 2)(task_keys)
        pl.when(t == last + 3)(task_inputs)
        for step in range(5):
            pl.when(t == last + 4 + step)(functools.partial(task_gain, step))

    lefts = (hidden, normed_ff, normed_ff, attended, normed_in, normed_in)
    rights = (grad_ff_proj, grad_gate, grad_up, grad_attn_proj, grad_query, grad_kv)
    reduce_steps(r, lefts, rights, dim, depth, x, core, z, y, sibling, beside, across, line, tasks)

    gain_gather().wait_send()
    for i in range(len(items)):
        first(i).wait_send()
        second(i).wait_send()
        third(i, x, 2).wait_send()
        third(i, 1 - x, 3).wait_send()
    for d in range(1, hops + 1):
        @pl.when(there(d))
        def _(d=d):
            for k in range(3):
                shift_copy(k, d).wait_send()

        @pl.when(there(-d))
        def _(d=d):
            for k in range(2):
                back_copy(k, d).wait_send()
    for step in range(2 + depth):
        gain_copy(step).wait_send()


def term_groups(lefts, rights, dim, depth):
    groups = []
    for left, right in zip(lefts, rights):
        columns = right.shape[1]
        by_columns = columns % (depth * LANES) == 0
        piece = dim // 8 * LANES
        if by_columns:
            chunks = columns // (depth * LANES)
        else:
            chunks = left.shape[1] * columns // (8 * depth * piece)
        groups.append((left, right, by_columns, chunks))
    return groups


def reduce_steps(
    r, lefts, rights, dim, depth, x, core, z, y, sibling, beside, across, line, tasks
):
    terms, out = r.terms, r.summed
    from_core, from_across, from_beside, from_line = (
        r.from_core, r.from_across, r.from_beside, r.from_line
    )
    chunks = terms.shape[0]
    piece_rows = terms.shape[5]

    def to_core(c):
        send, recv = r.sem_core
        return remote(terms.at[c, 1 - core], from_core.at[c], send.at[c], recv.at[c], sibling)

    def to_across(c):
        send, recv = r.sem_across
        return remote(from_core.at[c, 1 - y], from_across.at[c], send.at[c], recv.at[c], across)

    def to_beside(c):
        send, recv = r.sem_beside
        return remote(from_across.at[c, 1 - x], from_beside.at[c], send.at[c], recv.at[c], beside)

    def to_line(c, d):
        send, recv = r.sem_line
        return remote(
            from_beside.at[c, lax.rem(z + d, depth)], from_line.at[c, d - 1],
            send.at[c, d - 1], recv.at[c, d - 1], line[d - 1],
        )

    def along_line(c, d, arrival=False):
        send, recv = r.sem_zline
        block = out.at[c, core, x, lax.rem(z + depth - d, depth) if arrival else z]
        return remote(block, block, send.at[c, d - 1], recv.at[c, d - 1], line[d - 1])

    def back_beside(c, side):
        send, recv = r.sem_xback
        block = out.at[c, core, side]
        return remote(block, block, send.at[c], recv.at[c], beside)

    def back_core(c, side):
        send, recv = r.sem_back
        block = out.at[c, side]
        return remote(block, block, send.at[c], recv.at[c], sibling)

    def make_columns(left, right, at, c):
        width = depth * LANES
        block = token_dot(left[...], right[:, lane_block(at, width)])
        for side in range(2):
            for own in range(2):
                for across_x in range(2):
                    low = ((side * 2 + own) * 2 + across_x) * piece_rows
                    for place in range(depth):
                        terms[c, own, side, across_x, place] = block[
                            low : low + piece_rows, place * LANES : (place + 1) * LANES
                        ]

    def make_rows(left, right, at, c, parts):
        rows, tiles = left.shape[1] // (2 * parts), right.shape[1] // LANES
        high = rows // (4 * depth)
        for side in range(2):
            start = pl.multiple_of((side * parts + at) * rows, rows)
            block = token_dot(left[:, pl.ds(start, rows)], right[...])
            for own in range(2):
                for across_x in range(2):
                    for place in range(depth):
                        low = ((own * 2 + across_x) * depth + place) * high
                        for tile in range(tiles):
                            terms[
                                c, own, side, across_x, place, tile * high : (tile + 1) * high
                            ] = block[low : low + high, tile * LANES : (tile + 1) * LANES]

    def make(t):
        start = 0
        for left, right, by_columns, parts in term_groups(lefts, rights, dim, depth):
            @pl.when((t >= start) & (t < start + parts))
            def _(left=left, right=right, by_columns=by_columns, parts=parts, start=start):
                if by_columns:
                    make_columns(left, right, t - start, t)
                else:
                    make_rows(left, right, t - start, t, parts)
            start += parts
        to_core(t).start()

    def stage(at, action):
        @pl.when((at >= 0) & (at < chunks))
        def _():
            action(at)

    def after_core(c):
        to_core(c).wait_recv()
        from_core[c, 1 - y] = add_bf16(from_core[c, 1 - y], terms[c, core, 1 - y])
        to_across(c).start()
        from_core[c, y] = add_bf16(from_core[c, y], terms[c, core, y])

    def after_across(c):
        to_across(c).wait_recv()
        from_across[c, 1 - x] = add_bf16(from_across[c, 1 - x], from_core[c, y, 1 - x])
        to_beside(c).start()
        from_across[c, x] = add_bf16(from_across[c, x], from_core[c, y, x])

    def after_beside(c):
        to_beside(c).wait_recv()
        from_beside[c] = add_bf16(from_beside[c], from_across[c, x])
        for d in range(1, depth):
            to_line(c, d).start()

    def after_line(c):
        total = from_beside[c, z].astype(jnp.float32)
        for d in range(1, depth):
            to_line(c, d).wait_recv()
            total = total + from_line[c, d - 1].astype(jnp.float32)
        out[c, core, x, z] = total.astype(jnp.bfloat16)
        for d in range(1, depth):
            along_line(c, d).start()

    def after_zline(c):
        for d in range(1, depth):
            along_line(c, d, True).wait_recv()
        back_beside(c, x).start()

    def after_xback(c):
        back_beside(c, 1 - x).wait_recv()
        back_core(c, core).start()

    actions = [make, after_core, after_across, after_beside, after_line, after_zline, after_xback]

    @pl.loop(0, chunks + len(actions) - 1)
    def _(t):
        for lag, action in enumerate(actions):
            stage(t - lag, action)
        tasks(t)

    @pl.loop(0, chunks)
    def _(c):
        back_core(c, 1 - core).wait_recv()
        to_core(c).wait_send()
        to_across(c).wait_send()
        to_beside(c).wait_send()
        for d in range(1, depth):
            to_line(c, d).wait_send()
            along_line(c, d).wait_send()
        back_beside(c, x).wait_send()
        back_core(c, core).wait_send()


def run_layer(x, cotangent, docs, cos_table, sin_table, gains_own, weights):
    rows, dim = x.shape
    depth = lax.axis_size("seq") // 4
    head_dim = weights.key.shape[1]
    inner = weights.query.shape[1]
    heads = inner // head_dim
    ff = weights.gate.shape[1]
    hops = WINDOW // rows
    keys = (hops + 1) * rows
    bf16, f32 = jnp.bfloat16, jnp.float32
    dma = pltpu.SemaphoreType.DMA
    chunks = (2 * inner * dim + 2 * dim * head_dim + 3 * dim * ff) // (dim * depth * LANES)
    piece = (dim // 8, LANES)
    item_count = 10
    gain_shape = (GAIN_ROWS, dim)
    pair = Sems(dma((chunks,)), dma((chunks,)))
    lines = Sems(dma((chunks, depth - 1)), dma((chunks, depth - 1)))
    fulls = [pltpu.VMEM((2 * w.shape[0], w.shape[1]), bf16) for w in weights]
    scratch = dict(
        gains_other=pltpu.VMEM(gain_shape, f32),
        gains=pltpu.VMEM(gain_shape, f32),
        halo_docs=pltpu.VMEM((hops,) + docs.shape, docs.dtype),
        bias=pltpu.VMEM((rows, keys), f32),
        normed_in=pltpu.VMEM((rows, dim), bf16),
        key_raw=pltpu.VMEM((rows, head_dim), f32),
        query_raw=pltpu.VMEM((rows, inner), f32),
        queries=pltpu.VMEM((rows, inner), bf16),
        all_keys=pltpu.VMEM((keys, head_dim), bf16),
        all_values=pltpu.VMEM((keys, head_dim), bf16),
        probs=pltpu.VMEM((heads, rows, keys), f32),
        attended=pltpu.VMEM((rows, inner), bf16),
        attn_proj=pltpu.VMEM((rows, dim), f32),
        resid=pltpu.VMEM((rows, dim), f32),
        normed_ff=pltpu.VMEM((rows, dim), bf16),
        slope=pltpu.VMEM((rows, ff), f32),
        act=pltpu.VMEM((rows, ff), f32),
        hidden=pltpu.VMEM((rows, ff), bf16),
        ff_proj=pltpu.VMEM((rows, dim), f32),
        grad_ff_proj=pltpu.VMEM((rows, dim), bf16),
        grad_gains=pltpu.VMEM(gain_shape, f32),
        grad_gate=pltpu.VMEM((rows, ff), bf16),
        grad_up=pltpu.VMEM((rows, ff), bf16),
        grad_attn_proj=pltpu.VMEM((rows, dim), bf16),
        grad_head=pltpu.VMEM((rows, head_dim), bf16),
        grad_score=pltpu.VMEM((rows, keys), bf16),
        grad_keys=pltpu.VMEM((keys, head_dim), f32),
        grad_values=pltpu.VMEM((keys, head_dim), f32),
        grad_query=pltpu.VMEM((rows, inner), bf16),
        grad_kv=pltpu.VMEM((rows, 2 * head_dim), bf16),
        back_send=pltpu.VMEM((2, hops * rows, head_dim), bf16),
        back_recv=pltpu.VMEM((2, hops, rows, head_dim), bf16),
        terms=pltpu.VMEM((chunks, 2, 2, 2, depth) + piece, bf16),
        from_core=pltpu.VMEM((chunks, 2, 2, depth) + piece, bf16),
        from_across=pltpu.VMEM((chunks, 2, depth) + piece, bf16),
        from_beside=pltpu.VMEM((chunks, depth) + piece, bf16),
        from_line=pltpu.VMEM((chunks, depth - 1) + piece, bf16),
        gain_in=pltpu.VMEM((2 + depth,) + gain_shape, f32),
        gain_steps=pltpu.VMEM((3,) + gain_shape, f32),
        gain_gather_sems=dma((2,)),
        own_sems=dma((len(weights),)),
        g_send=dma((4, item_count)),
        g_recv=dma((4, item_count)),
        shift_send=dma((3, hops)),
        shift_recv=dma((3, hops)),
        back_shift_send=dma((2, hops)),
        back_shift_recv=dma((2, hops)),
        send_gain=dma((2 + depth,)),
        recv_gain=dma((2 + depth,)),
        sem_core=pair,
        sem_across=pair,
        sem_beside=pair,
        sem_xback=pair,
        sem_back=pair,
        sem_line=lines,
        sem_zline=lines,
    )
    vmem = pl.BlockSpec(memory_space=pltpu.VMEM)
    return pl.pallas_call(
        functools.partial(layer_kernel, tuple(scratch)),
        out_shape=[
            jax.ShapeDtypeStruct((rows, dim), bf16),
            jax.ShapeDtypeStruct((rows, dim), f32),
            jax.ShapeDtypeStruct((chunks, 2, 2, depth) + piece, bf16),
            jax.ShapeDtypeStruct(gain_shape, f32),
        ],
        in_specs=[vmem] * 6 + [pl.BlockSpec(memory_space=pl.ANY)] * len(weights),
        out_specs=[vmem] * 4,
        scratch_shapes=fulls + list(scratch.values()),
        compiler_params=pltpu.CompilerParams(
            collective_id=1, has_side_effects=True, vmem_limit_bytes=67043328
        ),
        name="layer",
    )(x, cotangent, docs, cos_table, sin_table, gains_own, *weights)


def finish_kernel(plan, count, summed_in, layer_in, inputs_in, *refs):
    outs, layer_out, grad_inputs = refs[:count], refs[count], refs[count + 1]
    stages = refs[count + 2 : 2 * count + 2]
    summed, layer_stage, inputs_stage, chunk_sems, side_sems, in_sems = refs[2 * count + 2 :]
    chunks, depth, rows = summed.shape[0], summed.shape[3], summed.shape[4]

    def fetch(c):
        return pltpu.make_async_copy(summed_in.at[c], summed.at[c], in_sems.at[c])

    sides = [
        pltpu.make_async_copy(layer_in, layer_stage, in_sems.at[chunks]),
        pltpu.make_async_copy(inputs_in, inputs_stage, in_sems.at[chunks + 1]),
    ]
    puts = [
        pltpu.make_async_copy(layer_stage, layer_out, side_sems.at[0]),
        pltpu.make_async_copy(inputs_stage, grad_inputs, side_sems.at[1]),
    ]
    fetch(0).start()
    for copy in sides:
        copy.start()

    @pl.loop(1, chunks)
    def _(c):
        fetch(c).start()


    def copies(group, at):
        outputs, by_columns, start, parts = group
        if len(outputs) > 1:
            return [
                pltpu.make_async_copy(stages[k], outs[k], chunk_sems.at[start + n])
                for n, k in enumerate(outputs)
            ]
        stage, out = stages[outputs[0]], outs[outputs[0]]
        if by_columns:
            view = (slice(None), lane_block(at, depth * LANES))
        else:
            high = stage.shape[0] // parts
            view = (pl.ds(pl.multiple_of(at * high, high), high),)
        return [pltpu.make_async_copy(stage.at[view], out.at[view], chunk_sems.at[start + at])]

    def convert(group, at):
        outputs, by_columns, start, parts = group
        stage = stages[outputs[0]]
        fetch(start + at).wait()
        for core in range(2):
            for x in range(2):
                for z in range(depth):
                    piece = summed[start + at, core, x, z].astype(jnp.float32)
                    if by_columns:
                        low = (core * 2 + x) * rows
                        if len(outputs) > 1:
                            wide = stage.shape[1]
                            stage = stages[outputs[z * LANES // wide]]
                            place = pl.ds(z * LANES % wide, LANES)
                        else:
                            place = pl.ds(
                                pl.multiple_of(at * depth * LANES + z * LANES, LANES), LANES
                            )
                        stage[low : low + rows, place] = piece
                    else:
                        tiles = stage.shape[1] // LANES
                        high = rows // tiles
                        block = stage.shape[0] // parts
                        low = pl.multiple_of(
                            at * block + ((core * 2 + x) * depth + z) * high, high
                        )
                        for tile in range(tiles):
                            stage[pl.ds(low, high), tile * LANES : (tile + 1) * LANES] = piece[
                                tile * high : (tile + 1) * high
                            ]
        for copy in copies(group, at):
            copy.start()

    for copy, put in zip(sides, puts):
        copy.wait()
        put.start()
    for group in plan:
        if group[3] == 1:
            convert(group, 0)
        else:
            pl.loop(0, group[3])(functools.partial(convert, group))
    for group in plan:
        for at in range(group[3]):
            for copy in copies(group, at):
                copy.wait()
    for put in puts:
        put.wait()


def finish(summed, layer_out, grad_inputs, shapes):
    chunks, _, _, depth, rows, lanes = summed.shape
    width = depth * lanes
    plan, start, index = [], 0, 0
    while index < len(shapes):
        high, wide = shapes[index]
        together = max(1, width // wide) if wide <= width and width % wide == 0 else 1
        by_columns = (wide * together) % width == 0
        if by_columns:
            parts = wide * together // width
        else:
            parts = high * wide // (4 * depth * rows * lanes)
        plan.append((list(range(index, index + together)), by_columns, start, parts))
        start += parts
        index += together
    anywhere = pl.BlockSpec(memory_space=pl.ANY)
    results = [jax.ShapeDtypeStruct(shape, jnp.float32) for shape in shapes]
    return pl.pallas_call(
        functools.partial(finish_kernel, plan, len(shapes)),
        out_shape=results
        + [jax.ShapeDtypeStruct(a.shape, a.dtype) for a in (layer_out, grad_inputs)],
        in_specs=[anywhere] * 3,
        out_specs=[anywhere] * (len(shapes) + 2),
        scratch_shapes=[pltpu.VMEM(shape, jnp.float32) for shape in shapes]
        + [pltpu.VMEM(a.shape, a.dtype) for a in (summed, layer_out, grad_inputs)]
        + [
            pltpu.SemaphoreType.DMA((chunks + len(shapes),)),
            pltpu.SemaphoreType.DMA((2,)),
            pltpu.SemaphoreType.DMA((chunks + 2,)),
        ],
        compiler_params=pltpu.CompilerParams(vmem_limit_bytes=67043328),
        name="finish",
    )(summed, layer_out, grad_inputs)


def pack_gains(small, dim):
    me = lax.axis_index("wshard")
    row_at = lax.broadcasted_iota(jnp.int32, (GAIN_ROWS, dim), 0)
    packed = jnp.zeros((GAIN_ROWS, dim), jnp.float32)
    for row, vec in enumerate(small):
        n = vec.shape[0]
        vec = vec.astype(jnp.float32)
        spread = jnp.where(me == 0, jnp.pad(vec, (0, dim - n)), jnp.pad(vec, (n, dim - 2 * n)))
        wide = lax.broadcast_in_dim(spread, (GAIN_ROWS, dim), (1,))
        packed = jnp.where(row_at == row, wide, packed)
    return packed


def per_device(
    inputs, doc_ids, w_query, w_key, w_value, w_out, w_gate, w_up, w_down,
    gain_in, gain_attn_post, gain_ff_pre, gain_ff_post, gain_query, gain_key, cotangent,
):
    rows, dim = inputs.shape
    small = (gain_in, gain_attn_post, gain_ff_pre, gain_ff_post, gain_query, gain_key)
    start_row = lax.axis_index(("seq", "wshard")) * rows
    cos_table, sin_table = rope_tables(
        start_row + jnp.arange(rows, dtype=jnp.int32), w_key.shape[1]
    )
    layer_out, grad_inputs, summed, gain_sums = run_layer(
        inputs, cotangent, doc_ids.reshape(-1, LANES), cos_table, sin_table,
        pack_gains(small, dim), Weights(w_key, w_value, w_query, w_out, w_gate, w_up, w_down),
    )
    order = (w_down, w_gate, w_up, w_out, w_query, w_key, w_value)
    results = finish(summed, layer_out, grad_inputs, [w.shape for w in order])
    sum_down, sum_gate, sum_up, sum_out, sum_query, sum_key, sum_value = results[:7]
    layer_out, grad_inputs = results[7:]
    me = lax.axis_index("wshard")
    gain_outs = []
    for row, vec in enumerate(small):
        n = vec.shape[0]
        gain_outs.append(jnp.where(me == 0, gain_sums[row, :n], gain_sums[row, n : 2 * n]))
    return (
        layer_out, grad_inputs, sum_query, sum_key, sum_value, sum_out, sum_gate, sum_up, sum_down,
    ) + tuple(gain_outs)


def per_device_general(
    inputs,
    doc_ids,
    w_query,
    w_key,
    w_value,
    w_out,
    w_gate,
    w_up,
    w_down,
    gain_in,
    gain_attn_post,
    gain_ff_pre,
    gain_ff_post,
    gain_query,
    gain_key,
    cotangent,
):
    gathered = (
        lax.all_gather(w_query, "wshard", axis=0, tiled=True),
        lax.all_gather(w_key, "wshard", axis=0, tiled=True),
        lax.all_gather(w_value, "wshard", axis=0, tiled=True),
        lax.all_gather(w_out, "wshard", axis=0, tiled=True),
        lax.all_gather(w_gate, "wshard", axis=0, tiled=True),
        lax.all_gather(w_up, "wshard", axis=0, tiled=True),
        lax.all_gather(w_down, "wshard", axis=0, tiled=True),
        lax.all_gather(gain_in, "wshard", axis=0, tiled=True),
        lax.all_gather(gain_attn_post, "wshard", axis=0, tiled=True),
        lax.all_gather(gain_ff_pre, "wshard", axis=0, tiled=True),
        lax.all_gather(gain_ff_post, "wshard", axis=0, tiled=True),
        lax.all_gather(gain_query, "wshard", axis=0, tiled=True),
        lax.all_gather(gain_key, "wshard", axis=0, tiled=True),
    )
    full_query, full_key, full_value, full_out, full_gate, full_up, full_down = gathered[:7]
    in_gain, attn_post_gain, ff_pre_gain, ff_post_gain, query_gain, key_gain = [
        g.astype(jnp.float32) for g in gathered[7:]
    ]
    row_count = inputs.shape[0]
    head_dim = full_key.shape[1]
    head_count = full_query.shape[1] // head_dim
    score_scale = head_dim ** (-0.5)
    start_row = lax.axis_index(("seq", "wshard")) * row_count
    query_pos = start_row + jnp.arange(row_count, dtype=jnp.int32)
    cos_table, sin_table = rope_tables(query_pos, head_dim)
    x_float = inputs.astype(jnp.float32)
    normed_in = rms_gain(x_float, in_gain).astype(jnp.bfloat16)
    query_raw = jnp.dot(normed_in, full_query, preferred_element_type=jnp.float32).reshape(
        row_count, head_count, head_dim
    )
    key_raw = jnp.dot(normed_in, full_key, preferred_element_type=jnp.float32)[:, None, :]
    values = jnp.dot(normed_in, full_value, preferred_element_type=jnp.float32).astype(jnp.bfloat16)
    queries = norm_rope(query_raw, query_gain, cos_table, sin_table).astype(jnp.bfloat16)
    key_rot = norm_rope(key_raw, key_gain, cos_table, sin_table)[:, 0].astype(jnp.bfloat16)
    sent_rows = min(WINDOW, row_count)
    hop_count = WINDOW // sent_rows
    outgoing = (key_rot, values, doc_ids)
    halo_keys = []
    halo_values = []
    halo_docs = []
    for distance in range(hop_count, 0, -1):
        arrived = from_behind((outgoing[0], outgoing[1], outgoing[2]), ("seq", "wshard"), distance)
        halo_keys.append(arrived[0])
        halo_values.append(arrived[1])
        halo_docs.append(arrived[2])
    all_keys = jnp.concatenate(halo_keys + [key_rot], 0)
    all_values = jnp.concatenate(halo_values + [values], 0)
    all_docs = jnp.concatenate(halo_docs + [doc_ids], 0)
    key_pos = start_row - WINDOW + jnp.arange(WINDOW + row_count, dtype=jnp.int32)
    allowed = window_mask(query_pos, key_pos, doc_ids, all_docs)
    scores = masked_scores(queries, all_keys, allowed, score_scale)
    row_peak = jnp.max(scores, axis=-1, keepdims=True)
    row_total = jnp.sum(
        jnp.where(allowed[None], jnp.exp(scores - row_peak), 0.0), axis=-1, keepdims=True
    )
    log_total = row_peak + jnp.log(row_total)
    soft = jnp.where(allowed[None], jnp.exp(scores - log_total), 0.0).astype(jnp.bfloat16)
    attended = jnp.einsum("hqk,kd->qhd", soft, all_values, preferred_element_type=jnp.float32)
    attended = attended.reshape(row_count, head_count * head_dim).astype(jnp.bfloat16)
    attn_proj = jnp.dot(attended, full_out, preferred_element_type=jnp.float32)
    resid = x_float + rms_gain(attn_proj, attn_post_gain)
    normed_ff = rms_gain(resid, ff_pre_gain).astype(jnp.bfloat16)
    gate_pre = jnp.dot(normed_ff, full_gate, preferred_element_type=jnp.float32)
    up_pre = jnp.dot(normed_ff, full_up, preferred_element_type=jnp.float32)
    hidden = geglu(gate_pre, up_pre).astype(jnp.bfloat16)
    ff_proj = jnp.dot(hidden, full_down, preferred_element_type=jnp.float32)
    layer_out = (resid + rms_gain(ff_proj, ff_post_gain)).astype(jnp.bfloat16)
    grad_top = cotangent.astype(jnp.float32)
    _, pullback = jax.vjp(rms_gain, ff_proj, ff_post_gain)
    grad_ff_proj, grad_gain_ff_post = pullback(grad_top)
    grad_ff_proj = grad_ff_proj.astype(jnp.bfloat16)
    grad_w_down = weight_grad(hidden, grad_ff_proj)
    grad_hidden = lax.dot_general(
        grad_ff_proj, full_down, (((1,), (1,)), ((), ())), preferred_element_type=jnp.float32
    )
    _, pullback = jax.vjp(geglu, gate_pre, up_pre)
    grad_gate, grad_up = pullback(grad_hidden)
    grad_gate = grad_gate.astype(jnp.bfloat16)
    grad_up = grad_up.astype(jnp.bfloat16)
    grad_w_gate = weight_grad(normed_ff, grad_gate)
    grad_w_up = weight_grad(normed_ff, grad_up)
    grad_normed_ff = lax.dot_general(
        grad_gate, full_gate, (((1,), (1,)), ((), ())), preferred_element_type=jnp.float32
    )
    grad_normed_ff = grad_normed_ff + lax.dot_general(
        grad_up, full_up, (((1,), (1,)), ((), ())), preferred_element_type=jnp.float32
    )
    _, pullback = jax.vjp(rms_gain, resid, ff_pre_gain)
    grad_resid_part, grad_gain_ff_pre = pullback(grad_normed_ff)
    grad_resid = grad_top + grad_resid_part
    ff_gradients = (grad_w_gate, grad_w_up, grad_w_down, grad_gain_ff_pre, grad_gain_ff_post)
    ff_parts = (
        lax.psum_scatter(
            ff_gradients[0].astype(jnp.bfloat16), "wshard", scatter_dimension=0, tiled=True
        ).astype(jnp.float32),
        lax.psum_scatter(
            ff_gradients[1].astype(jnp.bfloat16), "wshard", scatter_dimension=0, tiled=True
        ).astype(jnp.float32),
        lax.psum_scatter(
            ff_gradients[2].astype(jnp.bfloat16), "wshard", scatter_dimension=0, tiled=True
        ).astype(jnp.float32),
        lax.psum_scatter(
            ff_gradients[3].astype(jnp.bfloat16), "wshard", scatter_dimension=0, tiled=True
        ).astype(jnp.float32),
        lax.psum_scatter(
            ff_gradients[4].astype(jnp.bfloat16), "wshard", scatter_dimension=0, tiled=True
        ).astype(jnp.float32),
    )
    ff_reduced = (
        lax.psum(ff_parts[0].astype(jnp.bfloat16), "seq").astype(jnp.float32),
        lax.psum(ff_parts[1].astype(jnp.bfloat16), "seq").astype(jnp.float32),
        lax.psum(ff_parts[2].astype(jnp.bfloat16), "seq").astype(jnp.float32),
        lax.psum(ff_parts[3].astype(jnp.bfloat16), "seq").astype(jnp.float32),
        lax.psum(ff_parts[4].astype(jnp.bfloat16), "seq").astype(jnp.float32),
    )
    _, pullback = jax.vjp(rms_gain, attn_proj, attn_post_gain)
    grad_attn_proj, grad_gain_attn_post = pullback(grad_resid)
    grad_attn_proj = grad_attn_proj.astype(jnp.bfloat16)
    grad_w_out = weight_grad(attended, grad_attn_proj)
    grad_attended = lax.dot_general(
        grad_attn_proj, full_out, (((1,), (1,)), ((), ())), preferred_element_type=jnp.float32
    ).astype(jnp.bfloat16)
    grad_heads = grad_attended.reshape(row_count, head_count, head_dim)
    again_scores = masked_scores(queries, all_keys, allowed, score_scale)
    probs = jnp.where(allowed[None], jnp.exp(again_scores - log_total), 0.0)
    grad_soft = jnp.einsum(
        "qhd,kd->hqk", grad_heads, all_values, preferred_element_type=jnp.float32
    )
    row_inner = jnp.sum(probs * grad_soft, axis=-1, keepdims=True)
    grad_score = (probs * (grad_soft - row_inner) * score_scale).astype(jnp.bfloat16)
    grad_queries = jnp.einsum(
        "hqk,kd->qhd", grad_score, all_keys, preferred_element_type=jnp.float32
    )
    grad_keys_all = jnp.einsum(
        "hqk,qhd->kd", grad_score, queries, preferred_element_type=jnp.float32
    )
    grad_values_all = jnp.einsum(
        "hqk,qhd->kd", probs.astype(jnp.bfloat16), grad_heads, preferred_element_type=jnp.float32
    )
    back_keys = jnp.zeros((sent_rows, head_dim), jnp.float32)
    back_values = jnp.zeros((sent_rows, head_dim), jnp.float32)
    for piece_index in range(hop_count):
        distance = hop_count - piece_index
        piece_start = piece_index * sent_rows
        arrived = (
            from_behind(
                grad_keys_all[piece_start : piece_start + sent_rows].astype(jnp.bfloat16),
                ("seq", "wshard"),
                -distance,
            ).astype(jnp.float32),
            from_behind(
                grad_values_all[piece_start : piece_start + sent_rows].astype(jnp.bfloat16),
                ("seq", "wshard"),
                -distance,
            ).astype(jnp.float32),
        )
        back_keys = back_keys + arrived[0]
        back_values = back_values + arrived[1]
    own_keys = grad_keys_all[WINDOW:]
    own_values = grad_values_all[WINDOW:]
    split_row = row_count - sent_rows
    grad_keys = jnp.concatenate([own_keys[:split_row], own_keys + back_keys], 0)
    grad_values = jnp.concatenate([own_values[:split_row], own_values + back_values], 0).astype(
        jnp.bfloat16
    )

    def query_path(tensor, gain_vec):
        return norm_rope(tensor, gain_vec, cos_table, sin_table)

    _, pullback = jax.vjp(query_path, query_raw, query_gain)
    grad_query_raw, grad_gain_query = pullback(grad_queries)
    _, pullback = jax.vjp(query_path, key_raw, key_gain)
    grad_key_raw, grad_gain_key = pullback(grad_keys[:, None, :])
    grad_query_raw = grad_query_raw.reshape(row_count, head_count * head_dim).astype(jnp.bfloat16)
    grad_key_raw = grad_key_raw[:, 0].astype(jnp.bfloat16)
    grad_w_query = weight_grad(normed_in, grad_query_raw)
    grad_w_key = weight_grad(normed_in, grad_key_raw)
    grad_w_value = weight_grad(normed_in, grad_values)
    grad_normed_in = lax.dot_general(
        grad_query_raw, full_query, (((1,), (1,)), ((), ())), preferred_element_type=jnp.float32
    )
    grad_normed_in = grad_normed_in + lax.dot_general(
        grad_key_raw, full_key, (((1,), (1,)), ((), ())), preferred_element_type=jnp.float32
    )
    grad_normed_in = grad_normed_in + lax.dot_general(
        grad_values, full_value, (((1,), (1,)), ((), ())), preferred_element_type=jnp.float32
    )
    _, pullback = jax.vjp(rms_gain, x_float, in_gain)
    grad_input_part, grad_gain_in = pullback(grad_normed_in)
    grad_inputs = grad_resid + grad_input_part
    attn_gradients = (
        grad_w_query,
        grad_w_key,
        grad_w_value,
        grad_w_out,
        grad_gain_in,
        grad_gain_attn_post,
        grad_gain_query,
        grad_gain_key,
    )
    attn_parts = (
        lax.psum_scatter(
            attn_gradients[0].astype(jnp.bfloat16), "wshard", scatter_dimension=0, tiled=True
        ).astype(jnp.float32),
        lax.psum_scatter(
            attn_gradients[1].astype(jnp.bfloat16), "wshard", scatter_dimension=0, tiled=True
        ).astype(jnp.float32),
        lax.psum_scatter(
            attn_gradients[2].astype(jnp.bfloat16), "wshard", scatter_dimension=0, tiled=True
        ).astype(jnp.float32),
        lax.psum_scatter(
            attn_gradients[3].astype(jnp.bfloat16), "wshard", scatter_dimension=0, tiled=True
        ).astype(jnp.float32),
        lax.psum_scatter(
            attn_gradients[4].astype(jnp.bfloat16), "wshard", scatter_dimension=0, tiled=True
        ).astype(jnp.float32),
        lax.psum_scatter(
            attn_gradients[5].astype(jnp.bfloat16), "wshard", scatter_dimension=0, tiled=True
        ).astype(jnp.float32),
        lax.psum_scatter(
            attn_gradients[6].astype(jnp.bfloat16), "wshard", scatter_dimension=0, tiled=True
        ).astype(jnp.float32),
        lax.psum_scatter(
            attn_gradients[7].astype(jnp.bfloat16), "wshard", scatter_dimension=0, tiled=True
        ).astype(jnp.float32),
    )
    attn_reduced = (
        lax.psum(attn_parts[0].astype(jnp.bfloat16), "seq").astype(jnp.float32),
        lax.psum(attn_parts[1].astype(jnp.bfloat16), "seq").astype(jnp.float32),
        lax.psum(attn_parts[2].astype(jnp.bfloat16), "seq").astype(jnp.float32),
        lax.psum(attn_parts[3].astype(jnp.bfloat16), "seq").astype(jnp.float32),
        lax.psum(attn_parts[4].astype(jnp.bfloat16), "seq").astype(jnp.float32),
        lax.psum(attn_parts[5].astype(jnp.bfloat16), "seq").astype(jnp.float32),
        lax.psum(attn_parts[6].astype(jnp.bfloat16), "seq").astype(jnp.float32),
        lax.psum(attn_parts[7].astype(jnp.bfloat16), "seq").astype(jnp.float32),
    )
    reduced = (
        attn_reduced[0],
        attn_reduced[1],
        attn_reduced[2],
        attn_reduced[3],
        ff_reduced[0],
        ff_reduced[1],
        ff_reduced[2],
        attn_reduced[4],
        attn_reduced[5],
        ff_reduced[3],
        ff_reduced[4],
        attn_reduced[6],
        attn_reduced[7],
    )
    return (layer_out, grad_inputs) + tuple(reduced)


def solution(mesh):
    routed = mesh.shape["wshard"] == 2 and mesh.shape["seq"] == 16
    return jax.shard_map(
        per_device if routed else per_device_general,
        mesh=mesh,
        in_specs=(
            P(("seq", "wshard"), None),
            P(("seq", "wshard")),
            P("wshard", None),
            P("wshard", None),
            P("wshard", None),
            P("wshard", None),
            P("wshard", None),
            P("wshard", None),
            P("wshard", None),
            P("wshard"),
            P("wshard"),
            P("wshard"),
            P("wshard"),
            P("wshard"),
            P("wshard"),
            P(("seq", "wshard"), None),
        ),
        out_specs=(
            P(("seq", "wshard"), None),
            P(("seq", "wshard"), None),
            P("wshard", None),
            P("wshard", None),
            P("wshard", None),
            P("wshard", None),
            P("wshard", None),
            P("wshard", None),
            P("wshard", None),
            P("wshard"),
            P("wshard"),
            P("wshard"),
            P("wshard"),
            P("wshard"),
            P("wshard"),
        ),
        check_vma=False,
    )
```
